256 devices in a mesh: tm: 32 (over x, y, core), row: 8 (over z).
Axes of the slice: x: 4, y: 4, z: 8, core: 2. Of those that a mesh axis runs over, the one named last changes fastest.
Arguments:
- frames_in: bfloat16 [64, 32, 64, 256], P('tm', 'row'), may hold values from -6 to 6
- cotangent: bfloat16 [64, 32, 64, 256], P('tm', 'row'), may hold values from -6 to 6
- kernel: bfloat16 [9, 256, 256], replicated, may hold values from -0.125 to 0.125
- readout: bfloat16 [256, 256], replicated, may hold values from -0.375 to 0.375
- feedthrough: float32 [256], replicated, may hold values from 0.5 to 1.5
- decay_rate: float32 [64, 256], P('tm'), may hold values from 0.05 to 1, as said below
- start_state: float32 [32, 64, 256], P('row'), may hold values from -6 to 6
Outputs:
- grad_frames: bfloat16 [64, 32, 64, 256], P('tm', 'row')
- grad_kernel: float32 [9, 256, 256], P(None, 'row')
- grad_readout: float32 [256, 256], P(None, 'row')
The draws below stay inside these ranges and needn't reach their ends.
Inputs may be any that keep to these rules, and one draw needn't show every extreme that they name: `decay_rate`: every entry lies strictly between 0 and 1.
All inputs are finite; a program needn't handle non-finite values.
Results may differ from the reference program's by a relative error of at most 0.015.
Values may be sent and summed in bfloat16 or wider, within the bound.
No kernel may reach another device: no remote copies, remote signals or barrier semaphores. Data moves between devices by JAX's collectives and lax.ppermute only.
A program may use at most 64 MiB of HBM per device.

```python
import math
import jax
import jax.numpy as jnp
from jax import lax

C = 256
P_SIZE = 256
WIDTH = 64
WINDOW_FRAMES = 64
HEIGHT = 32


def draw_decay_rate(key, part):
    key_slow = jax.random.fold_in(key, 11)
    key_pace = jax.random.fold_in(key, 12)
    key_quick = jax.random.fold_in(key, 13)
    key_jitter = jax.random.fold_in(key, 14)
    key_place = jax.random.fold_in(key, 15)
    key_depth = jax.random.fold_in(key, 16)
    slow_share = 0.5
    slow_mask = jax.random.bernoulli(key_slow, slow_share, (P_SIZE,))
    slow_pace = jnp.exp(jax.random.uniform(key_pace, (P_SIZE,), jnp.float32, math.log(0.1), math.log(1.0))) / WINDOW_FRAMES
    quick_pace = jnp.exp(jax.random.uniform(key_quick, (P_SIZE,), jnp.float32, math.log(0.125), math.log(0.34)))
    baseline_speed = jnp.where(slow_mask, slow_pace, quick_pace)
    random_wobble = jnp.exp(jax.random.uniform(key_jitter, (WINDOW_FRAMES, P_SIZE), jnp.float32, -0.7, 0.7))
    positions = jax.random.randint(key_place, (3,), 0, WINDOW_FRAMES)
    sudden_spike = jnp.any(jnp.arange(WINDOW_FRAMES)[:, None] == positions[None, :], axis=1)
    stack_depth = jax.random.uniform(key_depth, (WINDOW_FRAMES, 1), jnp.float32, 0.6, 0.85)
    final_output = jnp.exp(-baseline_speed[None, :] * random_wobble) * jnp.where(sudden_spike[:, None], stack_depth, 1.0)
    return final_output.astype(jnp.float32)


def spiked(entries, key, source, target, blocks, factor):
    def block_of(position):
        return (jnp.arange(entries.shape[position]) // (entries.shape[position] // blocks)).reshape((-1,) + (1,) * (entries.ndim - 1 - position))

    one_side = jax.random.permutation(key, blocks)[block_of(target)]
    other_side = (block_of(target) + blocks // 2) % blocks
    return jnp.where((block_of(source) == one_side) | (block_of(source) == other_side), factor * entries, entries)


def shard_levels(rng, shape, split, low, top_value):
    def one(position, shards_of):
        steps = jax.random.uniform(jax.random.fold_in(jax.random.fold_in(rng, 6), position), (shards_of,), jnp.float32, low / len(split), top_value / len(split))
        return jnp.repeat(jnp.exp(steps), shape[position] // shards_of).reshape((-1,) + (1,) * (len(shape) - position - 1))

    factor_of = one(*split[0])
    for cut in split[1:]:
        factor_of = factor_of * one(*cut)
    return factor_of


def centred(stream_key, dims, width, most, cuts=(), dtype=jnp.bfloat16):
    entries = width * jax.random.normal(stream_key, dims, jnp.float32)
    if cuts:
        entries = entries * shard_levels(stream_key, dims, cuts, -0.22, 0.18)
    return jnp.clip(entries, -most, most).astype(dtype)


def gaussian_with(stream_key, dims, scale, limit, split, heavy, kind=jnp.bfloat16):
    result = scale * jax.random.normal(stream_key, dims, jnp.float32)
    if split:
        result = result * shard_levels(stream_key, dims, split, -0.22, 0.18)
    return jnp.clip(spiked(result, jax.random.fold_in(stream_key, 3), *heavy), -limit, limit).astype(kind)


def setup_inputs(seed: int = 0) -> dict:
    keys = jax.random.split(jax.random.key(seed), 8)
    return {
        "frames_in": gaussian_with(keys[0], (WINDOW_FRAMES, HEIGHT, WIDTH, C), 1.0, 6.0, ((0, 32), (1, 8)), (1, 3, 8, 2.0)),
        "cotangent": centred(keys[1], (WINDOW_FRAMES, HEIGHT, WIDTH, C), 1.0, 6.0, ((0, 32), (1, 8))),
        "kernel": centred(keys[2], (9, C, P_SIZE), (9 * C) ** -0.5, 0.125),
        "readout": centred(keys[3], (P_SIZE, C), P_SIZE ** -0.5, 0.375),
        "feedthrough": jnp.clip(jax.random.uniform(keys[4], (C,), jnp.float32, 0.5, 1.5), 0.5, 1.5),
        "decay_rate": draw_decay_rate(jax.random.fold_in(keys[7], 71), 0),
        "start_state": centred(keys[6], (HEIGHT, WIDTH, P_SIZE), 1.0, 6.0, ((0, 8),), jnp.float32),
    }


SQRT_TWO_PI = 0.7978845608
CUBIC = 0.044715

def gelu_slope(mixture):
    inside = SQRT_TWO_PI * (mixture + CUBIC * mixture * mixture * mixture)
    tangent = jnp.tanh(inside)
    return 0.5 * (1.0 + tangent) + 0.5 * mixture * (1.0 - tangent * tangent) * SQRT_TWO_PI * (1.0 + 3.0 * CUBIC * mixture * mixture)

def frame_taps(padded, height, grid_width, flipped):
    pieces = []
    for vertical in range(3):
        for lateral in range(3):
            from_top = 2 - vertical if flipped else vertical
            from_left = 2 - lateral if flipped else lateral
            pieces.append(padded[from_top:from_top + height, from_left:from_left + grid_width, :])
    return jnp.stack(pieces, axis=2).reshape(height * grid_width, 9 * padded.shape[2])

def reference(frames_in, cotangent, kernel, readout, feedthrough, decay_rate, start_state):
    frame_total, height, grid_width, channels = frames_in.shape
    state_width = kernel.shape[2]
    points = height * grid_width
    forward_mat = kernel.reshape(9 * channels, state_width)
    backward_mat = jnp.transpose(kernel, (0, 2, 1)).reshape(9 * state_width, channels)
    gain_all = jnp.sqrt(1.0 - decay_rate * decay_rate)

    def advance(carried, inputs):
        frame_in, rate_now, gain_now = inputs
        padded = jnp.pad(frame_in, ((1, 1), (1, 1), (0, 0)))
        driven = jnp.dot(frame_taps(padded, height, grid_width, False), forward_mat, preferred_element_type=jnp.float32)
        carried = rate_now * carried + gain_now * driven.reshape(height, grid_width, state_width)
        return (carried, carried.astype(jnp.bfloat16))
    _, stored = lax.scan(advance, start_state, (frames_in, decay_rate, gain_all))
    later_rate = jnp.concatenate([decay_rate[1:], jnp.ones((1, state_width), jnp.float32)], axis=0)

    def retreat(carried, inputs):
        adjoint_next, kernel_sum, readout_sum = carried
        frame_in, upstream, states_bf, rate_next, gain_now = inputs
        flat_states = states_bf.reshape(points, state_width)
        mixture = jnp.dot(flat_states, readout, preferred_element_type=jnp.float32)
        slope_bf = (upstream.reshape(points, channels).astype(jnp.float32) * gelu_slope(mixture)).astype(jnp.bfloat16)
        pulled = jnp.dot(slope_bf, readout.T, preferred_element_type=jnp.float32)
        adjoint = pulled.reshape(height, grid_width, state_width) + rate_next * adjoint_next
        grad_drive = (gain_now * adjoint).astype(jnp.bfloat16)
        padded_drive = jnp.pad(grad_drive, ((1, 1), (1, 1), (0, 0)))
        spread = jnp.dot(frame_taps(padded_drive, height, grid_width, True), backward_mat, preferred_element_type=jnp.float32)
        grad_frame = (spread.reshape(height, grid_width, channels) + feedthrough * upstream.astype(jnp.float32)).astype(jnp.bfloat16)
        input_taps = frame_taps(jnp.pad(frame_in, ((1, 1), (1, 1), (0, 0))), height, grid_width, False)
        kernel_sum = kernel_sum + jnp.dot(input_taps.T, grad_drive.reshape(points, state_width), preferred_element_type=jnp.float32)
        readout_sum = readout_sum + jnp.dot(flat_states.T, slope_bf, preferred_element_type=jnp.float32)
        return ((adjoint, kernel_sum, readout_sum), grad_frame)
    initial = (jnp.zeros((height, grid_width, state_width), jnp.float32), jnp.zeros((9 * channels, state_width), jnp.float32), jnp.zeros((state_width, channels), jnp.float32))
    (_, kernel_sum, readout_sum), grad_frames = lax.scan(retreat, initial, (frames_in, cotangent, stored, later_rate, gain_all), reverse=True)
    scaling = 1.0 / math.sqrt(frame_total * height * grid_width)
    return (grad_frames, (kernel_sum * scaling).reshape(9, channels, state_width), readout_sum * scaling)
```

```python
import functools
import math

import jax
import jax.numpy as jnp
from jax import lax
from jax.experimental import pallas as pl
from jax.experimental.pallas import tpu as pltpu
from jax.sharding import PartitionSpec as P

SQRT_TWO_PI = 0.7978845608
CUBIC = 0.044715
BF = jnp.bfloat16
F32 = jnp.float32
PAD = 8
CELLS = ((0, 0), (0, 1), (2, 0), (2, 1), (1, 0), (1, 1), (3, 0), (3, 1))
VMEM = pl.BlockSpec(memory_space=pltpu.VMEM)


def call(body, name, outs, ins, scratch, flops=1 << 20, moved=1 << 20):
    many = isinstance(outs, (list, tuple))
    return pl.pallas_call(
        body,
        name=name,
        out_shape=outs,
        in_specs=[VMEM] * ins,
        out_specs=[VMEM] * len(outs) if many else VMEM,
        scratch_shapes=scratch,
        cost_estimate=pl.CostEstimate(flops=flops, bytes_accessed=moved, transcendentals=0),
        compiler_params=pltpu.CompilerParams(vmem_limit_bytes=40 << 20),
    )


def split3(value):
    high = value.astype(BF).astype(F32)
    rest = value - high
    middle = rest.astype(BF).astype(F32)
    return high, middle, rest - middle


def sublane(shape):
    return lax.broadcasted_iota(jnp.int32, shape, len(shape) - 2)


def gelu_slope(mixture):
    inside = SQRT_TWO_PI * (mixture + CUBIC * mixture * mixture * mixture)
    tangent = jnp.tanh(inside)
    return 0.5 * (1.0 + tangent) + 0.5 * mixture * (1.0 - tangent * tangent) * SQRT_TWO_PI * (
        1.0 + 3.0 * CUBIC * mixture * mixture
    )


def halo_body(frames, cotangent, start, out, parts):
    wide = frames.shape[2]
    for f in range(2):
        for row in range(2):
            out[pl.ds((2 * f + row) * wide, wide), :] = frames[f, 2 + row]
        out[pl.ds((4 + f) * wide, wide), :] = cotangent[f, 3]
    for place, piece in enumerate(split3(start[3])):
        parts[pl.ds(2 * place, 2), :] = piece
    parts[6:8, :] = jnp.zeros_like(parts[6:8, :])
    out[pl.ds(6 * wide, 8), :] = parts[...].astype(BF)


def spread_body(frames, cotangent, decay, halo, out, grid, slopes, parts):
    wide = frames.shape[2]
    for f in range(2):
        for row in range(6):
            grid[f, row, 0:PAD, :] = jnp.zeros((PAD, grid.shape[3]), F32)
            grid[f, row, PAD + wide :, :] = jnp.zeros((PAD, grid.shape[3]), F32)
            source = halo[pl.ds((2 * f + row) * wide, wide), :] if row < 2 else frames[f, row - 2]
            grid[f, row, PAD : PAD + wide, :] = source.astype(F32)
        for row in range(4):
            source = halo[pl.ds((4 + f) * wide, wide), :] if row < 1 else cotangent[f, row - 1]
            slopes[f, row, PAD : PAD + wide, :] = source.astype(F32)
    for place, piece in enumerate(split3(decay[...])):
        parts[pl.ds(2 * place, 2), :] = piece
    parts[6:8, :] = jnp.zeros_like(parts[6:8, :])
    rates = parts[...].astype(BF)
    step = sublane((8, grid.shape[3]))
    for target in range(wide // 2):
        first = PAD + 2 * target
        for f in range(2):
            for pair in range(3):
                begin = first - 1
                block = jnp.where(
                    step < 4,
                    grid[f, 2 * pair, begin : begin + 8, :],
                    grid[f, 2 * pair + 1, begin - 4 : begin + 4, :],
                )
                out[target, 32 * f + 8 * pair : 32 * f + 8 * pair + 8, :] = block.astype(BF)
            block = slopes[f, 0, first : first + 8, :]
            for place, row in ((2, 2), (4, 1), (6, 3)):
                block = jnp.where(step < place, block, slopes[f, row, first - place : first - place + 8, :])
            out[target, 32 * f + 24 : 32 * f + 32, :] = block.astype(BF)
        out[target, 64:72, :] = rates


def cell_body(
    got, kernel, readout, start, halo, out, grid, decay, gain, taps, driven, states, slopes, drive, turned, begin
):
    sources = got.shape[0]
    count = sources * 16
    wide = (halo.shape[0] - 8) // 6
    lanes = got.shape[2]
    step = sublane((8, lanes))
    is_first = lax.axis_index("row") == 0
    low = jnp.where(is_first & (step < 2), 0.0, 1.0)
    high = jnp.where(is_first & (step >= 4) & (step < 6), 0.0, 1.0)
    near = (step % 4) < 2

    def unpack(source, _):
        for f in range(2):
            grid[2 * source + f] = got[source, 32 * f : 32 * f + 24, :].astype(F32)
        piece = got[source, 64:72, :].astype(F32)
        rate = piece + pltpu.roll(piece, 6, 0) + pltpu.roll(piece, 4, 0)
        decay[source] = rate
        gain[source] = jnp.sqrt(1.0 - rate * rate)
        return _

    lax.fori_loop(0, sources, unpack, 0, unroll=4)

    def gather(source, _):
        rows = pl.ds(pl.multiple_of(16 * source, 16), 16)
        for i in range(3):
            for j in range(3):
                place = 4 * i + j
                pair = []
                for f in range(2):
                    value = jnp.where(
                        near,
                        grid[2 * source + f, place : place + 8, :],
                        grid[2 * source + f, place + 6 : place + 14, :],
                    )
                    if i == 2:
                        value = value * low
                    if i == 0:
                        value = value * high
                    pair.append(value)
                tap = 3 * i + j
                taps[rows, lanes * tap : lanes * tap + lanes] = jnp.concatenate(pair, axis=0).astype(BF)
        return _

    lax.fori_loop(0, sources, gather, 0, unroll=2)

    chunk = min(count, 256)

    def convolve(part, _):
        rows = pl.ds(pl.multiple_of(part * chunk, chunk), chunk)
        driven[rows, :] = jnp.dot(taps[rows, :], kernel[...], preferred_element_type=F32)
        return _

    lax.fori_loop(0, count // chunk, convolve, 0)

    tail = halo[6 * wide : 6 * wide + 8, :].astype(F32)
    begin[0:8, :] = tail
    top = begin[0:2, :] + begin[2:4, :] + begin[4:6, :]
    begin[0:2, :] = top
    begin[2:4, :] = start[1]
    begin[4:6, :] = start[0]
    begin[6:8, :] = start[2]

    def advance(source, state):
        pair = []
        for f in range(2):
            rate = jnp.broadcast_to(decay[source, f : f + 1, :], state.shape)
            size = jnp.broadcast_to(gain[source, f : f + 1, :], state.shape)
            now = driven[pl.ds(pl.multiple_of(16 * source + 8 * f, 8), 8), :]
            state = rate * state + size * now
            pair.append(state)
        states[pl.ds(pl.multiple_of(16 * source, 16), 16), :] = jnp.concatenate(pair, axis=0).astype(BF)
        return state

    lax.fori_loop(0, sources, advance, begin[...], unroll=4)

    def mix(part, _):
        rows = pl.ds(pl.multiple_of(part * 64, 64), 64)
        mixture = jnp.dot(states[rows, :], readout[...], preferred_element_type=F32)
        upstream = jnp.concatenate(
            [
                got[4 * part + source, 32 * f + 24 : 32 * f + 32, :].astype(F32)
                for source in range(4)
                for f in range(2)
            ],
            axis=0,
        )
        slope = (upstream * gelu_slope(mixture)).astype(BF)
        slopes[rows, :] = slope
        driven[rows, :] = lax.dot_general(
            slope, readout[...], (((1,), (1,)), ((), ())), preferred_element_type=F32
        )
        return _

    lax.fori_loop(0, count // 64, mix, 0, unroll=2)

    def retreat(turn, carried):
        adjoint, later = carried
        source = sources - 1 - turn
        pair = []
        for f in (1, 0):
            now = driven[pl.ds(pl.multiple_of(16 * source + 8 * f, 8), 8), :]
            adjoint = now + later * adjoint
            later = jnp.broadcast_to(decay[source, f : f + 1, :], adjoint.shape)
            value = jnp.broadcast_to(gain[source, f : f + 1, :], adjoint.shape) * adjoint
            pair.append(value)
            out[source, 0:8, 10 * lanes + f * lanes : 11 * lanes + f * lanes] = value.astype(BF)
        drive[pl.ds(pl.multiple_of(16 * source, 16), 16), :] = jnp.concatenate(pair[::-1], axis=0)
        return adjoint, later

    nothing = jnp.zeros((8, lanes), F32)
    lax.fori_loop(0, sources, retreat, (nothing, nothing), unroll=4)

    turned[...] = drive[...].astype(BF).T
    share = lanes // sources
    for tap in range(9):
        term = jnp.dot(turned[...], taps[:, lanes * tap : lanes * tap + lanes], preferred_element_type=F32)
        out[:, :, lanes * tap : lanes * tap + lanes] = term.astype(BF).reshape(sources, share, lanes)
    term = jnp.dot(states[...].T, slopes[...], preferred_element_type=F32)
    out[:, :, 9 * lanes : 10 * lanes] = term.astype(BF).reshape(sources, share, lanes)


def join_body(bands, got, total, frames, cells, grid):
    sources, share, width = got.shape
    lanes = width // 12

    def add(source, carried):
        return carried + got[source, :, : 10 * lanes].astype(F32)

    sums = lax.fori_loop(0, sources, add, jnp.zeros((share, 10 * lanes), F32), unroll=2)
    block = lanes // bands
    for band in range(bands):
        total[band] = jnp.concatenate(
            [sums[:, lanes * k + block * band : lanes * k + block * band + block] for k in range(10)], axis=1
        )

    for f in range(2):
        for part in range(lanes // 128):
            for source in range(sources):
                first = (10 + f) * lanes + 128 * part
                cells[8 * source : 8 * source + 8, :] = got[source, 0:8, first : first + 128].astype(F32)
            for place, (row, column) in enumerate(CELLS):
                grid[pl.ds(column, sources, stride=2), :] = cells[pl.ds(place, sources, stride=8), :]
                if column == 1:
                    frames[f, row, :, 128 * part : 128 * part + 128] = grid[...].astype(BF)


def back_body(bands, drive, below, kernel, cotangent, feedthrough, out, grid, moved):
    wide = drive.shape[2]
    lanes = drive.shape[3]
    band = lax.axis_index("row")
    for row in range(6):
        keep = None
        if row == 0:
            keep = jnp.where(band == 0, 0.0, 1.0)
        if row == 5:
            keep = jnp.where(band == bands - 1, 0.0, 1.0)
        for f in range(2):
            source = (drive[f, row] if row < 4 else below[f, row - 4]).astype(F32)
            if keep is not None:
                source = source * keep
            grid[0:PAD, :] = jnp.zeros((PAD, lanes), F32)
            grid[PAD + wide :, :] = jnp.zeros((PAD, lanes), F32)
            grid[PAD : PAD + wide, :] = source
            for shift in range(3):
                moved[shift, f, row] = grid[PAD - 1 + shift : PAD - 1 + shift + wide, :].astype(BF)
    for f in range(2):
        for half in range(2):
            total = jnp.zeros((2 * wide, lanes), F32)
            for i in range(3):
                for j in range(3):
                    first = 2 - i + 2 * half
                    cells = moved[2 - j, f, first : first + 2].reshape(2 * wide, lanes)
                    total = total + lax.dot_general(
                        cells, kernel[3 * i + j], (((1,), (1,)), ((), ())), preferred_element_type=F32
                    )
            total = total.reshape(2, wide, lanes)
            for row in range(2):
                place = 2 * half + row
                out[f, place] = (total[row] + feedthrough[...] * cotangent[f, place].astype(F32)).astype(BF)


def sum_body(scaling, got, out):
    total = got[0]
    for band in range(1, got.shape[0]):
        total = total + got[band]
    total = total * scaling
    for target in range(out.shape[0]):
        out[target] = total


def last_body(got, kernel_out, readout_out):
    sources, share, width = got.shape
    turned = got[...].reshape(sources * share, width).T
    block = width // 10
    for k in range(9):
        kernel_out[k] = turned[block * k : block * k + block]
    readout_out[...] = turned[9 * block :]


def local(frames_in, cotangent, kernel, readout, feedthrough, decay_rate, start_state):
    here, band_rows, wide, lanes = frames_in.shape
    sources, bands = lax.axis_size("tm"), lax.axis_size("row")
    cells = sources * 16
    share = lanes // sources
    block = lanes // bands
    shape = jax.ShapeDtypeStruct
    down = [(i, (i + 1) % bands) for i in range(bands)]
    up = [((i + 1) % bands, i) for i in range(bands)]

    start = lax.dynamic_slice_in_dim(start_state, 2 * lax.axis_index("tm"), 2, 1)
    edge = call(
        halo_body, "halo", shape((6 * wide + 8, lanes), BF), 3, [pltpu.VMEM((8, lanes), F32)]
    )(frames_in, cotangent, start)
    edge = lax.ppermute(edge, "row", down)
    send = call(
        spread_body,
        "spread",
        shape((sources, 72, lanes), BF),
        4,
        [
            pltpu.VMEM((2, 6, wide + 2 * PAD, lanes), F32),
            pltpu.VMEM((2, 4, wide + 2 * PAD, lanes), F32),
            pltpu.VMEM((8, lanes), F32),
        ],
    )(frames_in, cotangent, decay_rate, edge)
    got = lax.all_to_all(send, "tm", 0, 0)
    send = call(
        cell_body,
        "cells",
        shape((sources, max(8, share), 12 * lanes), BF),
        5,
        [
            pltpu.VMEM((2 * sources, 24, lanes), F32),
            pltpu.VMEM((sources, 8, lanes), F32),
            pltpu.VMEM((sources, 8, lanes), F32),
            pltpu.VMEM((cells, 9 * lanes), BF),
            pltpu.VMEM((cells, lanes), F32),
            pltpu.VMEM((cells, lanes), BF),
            pltpu.VMEM((cells, lanes), BF),
            pltpu.VMEM((cells, lanes), F32),
            pltpu.VMEM((lanes, cells), BF),
            pltpu.VMEM((8, lanes), F32),
        ],
        flops=2 * cells * lanes * lanes * 21,
        moved=4 << 20,
    )(got, kernel.reshape(9 * lanes, lanes), readout, start, edge)
    got = lax.all_to_all(send, "tm", 0, 0)
    partial, drive = call(
        functools.partial(join_body, bands),
        "join",
        (shape((bands, share, 10 * block), F32), shape((2, 4, wide, lanes), BF)),
        1,
        [pltpu.VMEM((8 * sources, 128), F32), pltpu.VMEM((wide, 128), F32)],
    )(got)
    below = lax.ppermute(drive[:, :2], "row", up)
    partial = lax.all_to_all(partial, "row", 0, 0)
    scaling = 1.0 / math.sqrt(here * sources * band_rows * bands * wide)
    partial = call(
        functools.partial(sum_body, scaling), "sum", shape((sources, share, 10 * block), F32), 1, []
    )(partial)
    grad_frames = call(
        functools.partial(back_body, bands),
        "back",
        shape(frames_in.shape, BF),
        5,
        [
            pltpu.VMEM((wide + 2 * PAD, lanes), F32),
            pltpu.VMEM((3, 2, 6, wide, lanes), BF),
        ],
        flops=2 * cells * lanes * lanes * 9,
        moved=2 << 20,
    )(drive, below, kernel, cotangent, feedthrough.reshape(1, lanes))
    whole = lax.all_to_all(partial, "tm", 0, 0)
    grad_kernel, grad_readout = call(
        last_body, "last", (shape((9, block, lanes), F32), shape((block, lanes), F32)), 1, []
    )(whole)
    return grad_frames, grad_kernel, grad_readout.T


def solution(mesh):
    placed = (
        P("tm", "row", None, None),
        P("tm", "row", None, None),
        P(),
        P(),
        P(),
        P("tm", None),
        P("row", None, None),
    )
    return jax.shard_map(
        local,
        mesh=mesh,
        in_specs=placed,
        out_specs=(P("tm", "row", None, None), P(None, "row", None), P(None, "row")),
        check_vma=False,
    )
```

```python
import functools
import math

import jax
import jax.numpy as jnp
from jax import lax
from jax.experimental import pallas as pl
from jax.experimental.pallas import tpu as pltpu
from jax.sharding import PartitionSpec as P

SQRT_TWO_PI = 0.7978845608
CUBIC = 0.044715
BF = jnp.bfloat16
F32 = jnp.float32
PAD = 8
CELLS = ((0, 0), (0, 1), (2, 0), (2, 1), (1, 0), (1, 1), (3, 0), (3, 1))
VMEM = pl.BlockSpec(memory_space=pltpu.VMEM)
HBM = pl.BlockSpec(memory_space=pltpu.MemorySpace.HBM)


def call(body, name, outs, ins, scratch, flops=1 << 20, moved=1 << 20, grant=40 << 20):
    many = isinstance(outs, (list, tuple))
    return pl.pallas_call(
        body,
        name=name,
        out_shape=outs,
        in_specs=ins,
        out_specs=[VMEM] * len(outs) if many else VMEM,
        scratch_shapes=scratch,
        cost_estimate=pl.CostEstimate(flops=flops, bytes_accessed=moved, transcendentals=0),
        compiler_params=pltpu.CompilerParams(vmem_limit_bytes=grant),
    )


def split3(value):
    high = value.astype(BF).astype(F32)
    rest = value - high
    middle = rest.astype(BF).astype(F32)
    return high, middle, rest - middle


def sublane(shape):
    return lax.broadcasted_iota(jnp.int32, shape, len(shape) - 2)


def gelu_slope(mixture):
    inside = SQRT_TWO_PI * (mixture + CUBIC * mixture * mixture * mixture)
    tangent = jnp.tanh(inside)
    return 0.5 * (1.0 + tangent) + 0.5 * mixture * (1.0 - tangent * tangent) * SQRT_TWO_PI * (
        1.0 + 3.0 * CUBIC * mixture * mixture
    )


def spread_body(frames, cotangent, decay, out, grid, slopes, rows, given, rates, parts, sems):
    wide, lanes = frames.shape[2:]
    copies = (
        pltpu.make_async_copy(frames, rows, sems.at[0]),
        pltpu.make_async_copy(cotangent, given, sems.at[1]),
        pltpu.make_async_copy(decay, rates, sems.at[2]),
    )
    for copy in copies:
        copy.start()
    for f in range(2):
        for row in range(4):
            grid[f, row, 0:PAD, :] = jnp.zeros((PAD, lanes), F32)
            grid[f, row, PAD + wide :, :] = jnp.zeros((PAD, lanes), F32)
    for copy in copies:
        copy.wait()
    for f in range(2):
        for row in range(4):
            grid[f, row, PAD : PAD + wide, :] = rows[f, row].astype(F32)
            slopes[f, row, PAD : PAD + wide, :] = given[f, row].astype(F32)
    for place, piece in enumerate(split3(rates[...])):
        parts[2 * place : 2 * place + 2, :] = piece
    parts[6:8, :] = jnp.zeros((2, lanes), F32)
    pieces = parts[...].astype(BF)
    step = sublane((8, lanes))
    for target in range(wide // 2):
        first = PAD + 2 * target
        for row in range(4):
            start = first - 1
            block = jnp.where(
                step < 4, grid[0, row, start : start + 8, :], grid[1, row, start - 4 : start + 4, :]
            )
            out[target, 8 * row : 8 * row + 8, :] = block.astype(BF)
        for f in range(2):
            block = slopes[f, 0, first : first + 8, :]
            for place, row in ((2, 2), (4, 1), (6, 3)):
                block = jnp.where(step < place, block, slopes[f, row, first - place : first - place + 8, :])
            out[target, 32 + 8 * f : 40 + 8 * f, :] = block.astype(BF)
        out[target, 48:56, :] = pieces


def cell_body(
    got,
    above,
    below,
    kernel,
    readout,
    start,
    out,
    grid,
    decay,
    gain,
    taps,
    driven,
    states,
    slopes,
    drive,
    turned,
    starts,
    sem,
):
    sources = got.shape[0]
    count = sources * 16
    lanes = got.shape[2]
    step = sublane((8, lanes))
    near = (step % 4) < 2
    mine = lax.axis_index("tm")
    fetch = pltpu.make_async_copy(start.at[:, pl.ds(pl.multiple_of(8 * (mine // 4), 8), 8)], starts, sem)
    fetch.start()

    def unpack(source, _):
        groups = [above[source], got[source, 0:8, :], got[source, 8:16, :]]
        groups += [got[source, 16:24, :], got[source, 24:32, :], below[source]]
        groups = [group.astype(F32) for group in groups]
        for pair in range(3):
            first, second = groups[2 * pair : 2 * pair + 2]
            rows = slice(8 * pair, 8 * pair + 8)
            grid[2 * source, rows, :] = jnp.where(step < 4, first, pltpu.roll(second, 4, 0))
            grid[2 * source + 1, rows, :] = jnp.where(step < 4, pltpu.roll(first, 4, 0), second)
        piece = got[source, 48:56, :].astype(F32)
        rate = piece + pltpu.roll(piece, 6, 0) + pltpu.roll(piece, 4, 0)
        decay[source] = rate
        gain[source] = jnp.sqrt(1.0 - rate * rate)
        return _

    lax.fori_loop(0, sources, unpack, 0, unroll=4)

    def gather(source, _):
        rows = pl.ds(pl.multiple_of(16 * source, 16), 16)
        for i in range(3):
            for j in range(3):
                place = 4 * i + j
                pair = []
                for f in range(2):
                    value = jnp.where(
                        near,
                        grid[2 * source + f, place : place + 8, :],
                        grid[2 * source + f, place + 6 : place + 14, :],
                    )
                    pair.append(value)
                tap = 3 * i + j
                taps[rows, lanes * tap : lanes * tap + lanes] = jnp.concatenate(pair, axis=0).astype(BF)
        return _

    lax.fori_loop(0, sources, gather, 0, unroll=2)

    chunk = min(count, 256)

    def convolve(part, _):
        rows = pl.ds(pl.multiple_of(part * chunk, chunk), chunk)
        driven[rows, :] = jnp.dot(taps[rows, :], kernel[...], preferred_element_type=F32)
        return _

    lax.fori_loop(0, count // chunk, convolve, 0)

    fetch.wait()
    offset = 2 * (mine % 4)
    begin = pltpu.roll(starts[0], (8 - offset) % 8, 0)
    for place, row in ((2, 2), (4, 1), (6, 3)):
        begin = jnp.where(step < place, begin, pltpu.roll(starts[row], (8 + place - offset) % 8, 0))

    def advance(source, state):
        pair = []
        for f in range(2):
            rate = jnp.broadcast_to(decay[source, f : f + 1, :], state.shape)
            size = jnp.broadcast_to(gain[source, f : f + 1, :], state.shape)
            now = driven[pl.ds(pl.multiple_of(16 * source + 8 * f, 8), 8), :]
            state = rate * state + size * now
            pair.append(state)
        states[pl.ds(pl.multiple_of(16 * source, 16), 16), :] = jnp.concatenate(pair, axis=0).astype(BF)
        return state

    lax.fori_loop(0, sources, advance, begin, unroll=4)

    def mix(part, _):
        rows = pl.ds(pl.multiple_of(part * 64, 64), 64)
        mixture = jnp.dot(states[rows, :], readout[...], preferred_element_type=F32)
        upstream = jnp.concatenate(
            [
                got[4 * part + source, 32 + 8 * f : 40 + 8 * f, :].astype(F32)
                for source in range(4)
                for f in range(2)
            ],
            axis=0,
        )
        slope = (upstream * gelu_slope(mixture)).astype(BF)
        slopes[rows, :] = slope
        driven[rows, :] = lax.dot_general(
            slope, readout[...], (((1,), (1,)), ((), ())), preferred_element_type=F32
        )
        return _

    lax.fori_loop(0, count // 64, mix, 0, unroll=2)

    def retreat(turn, carried):
        adjoint, later = carried
        source = sources - 1 - turn
        pair = []
        for f in (1, 0):
            now = driven[pl.ds(pl.multiple_of(16 * source + 8 * f, 8), 8), :]
            adjoint = now + later * adjoint
            later = jnp.broadcast_to(decay[source, f : f + 1, :], adjoint.shape)
            value = jnp.broadcast_to(gain[source, f : f + 1, :], adjoint.shape) * adjoint
            pair.append(value)
            out[source, 0:8, 10 * lanes + f * lanes : 11 * lanes + f * lanes] = value.astype(BF)
        drive[pl.ds(pl.multiple_of(16 * source, 16), 16), :] = jnp.concatenate(pair[::-1], axis=0)
        return adjoint, later

    nothing = jnp.zeros((8, lanes), F32)
    lax.fori_loop(0, sources, retreat, (nothing, nothing), unroll=4)

    turned[...] = drive[...].astype(BF).T
    share = lanes // sources
    for tap in range(9):
        term = jnp.dot(turned[...], taps[:, lanes * tap : lanes * tap + lanes], preferred_element_type=F32)
        out[:, :, lanes * tap : lanes * tap + lanes] = term.astype(BF).reshape(sources, share, lanes)
    term = jnp.dot(states[...].T, slopes[...], preferred_element_type=F32)
    out[:, :, 9 * lanes : 10 * lanes] = term.astype(BF).reshape(sources, share, lanes)


def join_body(bands, got, total, frames, top, bottom, cells, grid):
    sources, share, width = got.shape
    lanes = width // 12

    def add(source, carried):
        return carried + got[source, :, : 10 * lanes].astype(F32)

    sums = lax.fori_loop(0, sources, add, jnp.zeros((share, 10 * lanes), F32), unroll=2)
    block = lanes // bands
    for band in range(bands):
        total[band] = jnp.concatenate(
            [sums[:, lanes * k + block * band : lanes * k + block * band + block] for k in range(10)], axis=1
        )

    for f in range(2):
        for part in range(lanes // 128):
            for source in range(sources):
                first = (10 + f) * lanes + 128 * part
                cells[8 * source : 8 * source + 8, :] = got[source, 0:8, first : first + 128].astype(F32)
            for place, (row, column) in enumerate(CELLS):
                grid[pl.ds(column, sources, stride=2), :] = cells[pl.ds(place, sources, stride=8), :]
                if column == 1:
                    value = grid[...].astype(BF)
                    frames[f, row, :, 128 * part : 128 * part + 128] = value
                    if row == 0:
                        top[f, :, 128 * part : 128 * part + 128] = value
                    if row == 3:
                        bottom[f, :, 128 * part : 128 * part + 128] = value


def back_body(drive, above, below, kernel, cotangent, feedthrough, out, grid, moved):
    wide = drive.shape[2]
    lanes = drive.shape[3]
    for row in range(6):
        for f in range(2):
            if row == 0:
                source = above[f]
            elif row == 5:
                source = below[f]
            else:
                source = drive[f, row - 1]
            grid[0:PAD, :] = jnp.zeros((PAD, lanes), F32)
            grid[PAD + wide :, :] = jnp.zeros((PAD, lanes), F32)
            grid[PAD : PAD + wide, :] = source.astype(F32)
            for shift in range(3):
                moved[shift, f, row] = grid[PAD - 1 + shift : PAD - 1 + shift + wide, :].astype(BF)
    for f in range(2):
        for half in range(2):
            total = jnp.zeros((2 * wide, lanes), F32)
            for i in range(3):
                for j in range(3):
                    first = 2 - i + 2 * half
                    cells = moved[2 - j, f, first : first + 2].reshape(2 * wide, lanes)
                    total = total + lax.dot_general(
                        cells, kernel[3 * i + j], (((1,), (1,)), ((), ())), preferred_element_type=F32
                    )
            total = total.reshape(2, wide, lanes)
            for row in range(2):
                place = 2 * half + row
                out[f, place] = (total[row] + feedthrough[...] * cotangent[f, place].astype(F32)).astype(BF)


def sum_body(scaling, got, out):
    total = got[0]
    for band in range(1, got.shape[0]):
        total = total + got[band]
    total = total * scaling
    for target in range(out.shape[0]):
        out[target] = total


def last_body(got, kernel_out, readout_out):
    sources, share, width = got.shape
    turned = got[...].reshape(sources * share, width).T
    block = width // 10
    for k in range(9):
        kernel_out[k] = turned[block * k : block * k + block]
    readout_out[...] = turned[9 * block :]


def local(frames_in, cotangent, kernel, readout, feedthrough, decay_rate, start_state):
    here, band_rows, wide, lanes = frames_in.shape
    sources, bands = lax.axis_size("tm"), lax.axis_size("row")
    cells = sources * 16
    share = lanes // sources
    block = lanes // bands
    shape = jax.ShapeDtypeStruct
    down = [(i, i + 1) for i in range(bands - 1)]
    up = [(i + 1, i) for i in range(bands - 1)]

    send = call(
        spread_body,
        "spread",
        shape((sources, 56, lanes), BF),
        [HBM] * 3,
        [
            pltpu.VMEM((2, 4, wide + 2 * PAD, lanes), F32),
            pltpu.VMEM((2, 4, wide + 2 * PAD, lanes), F32),
            pltpu.VMEM((2, 4, wide, lanes), BF),
            pltpu.VMEM((2, 4, wide, lanes), BF),
            pltpu.VMEM((2, lanes), F32),
            pltpu.VMEM((8, lanes), F32),
            pltpu.SemaphoreType.DMA((3,)),
        ],
        grant=63 << 20,
    )(frames_in, cotangent, decay_rate)
    got = lax.all_to_all(send, "tm", 0, 0)
    above = lax.ppermute(got[:, 24:32], "row", down)
    below = lax.ppermute(got[:, 0:8], "row", up)
    send = call(
        cell_body,
        "cells",
        shape((sources, max(8, share), 12 * lanes), BF),
        [VMEM] * 5 + [HBM],
        [
            pltpu.VMEM((2 * sources, 24, lanes), F32),
            pltpu.VMEM((sources, 8, lanes), F32),
            pltpu.VMEM((sources, 8, lanes), F32),
            pltpu.VMEM((cells, 9 * lanes), BF),
            pltpu.VMEM((cells, lanes), F32),
            pltpu.VMEM((cells, lanes), BF),
            pltpu.VMEM((cells, lanes), BF),
            pltpu.VMEM((cells, lanes), F32),
            pltpu.VMEM((lanes, cells), BF),
            pltpu.VMEM((4, 8, lanes), F32),
            pltpu.SemaphoreType.DMA,
        ],
        flops=2 * cells * lanes * lanes * 21,
        moved=4 << 20,
    )(got, above, below, kernel.reshape(9 * lanes, lanes), readout, start_state)
    got = lax.all_to_all(send, "tm", 0, 0)
    edge = shape((2, wide, lanes), BF)
    partial, drive, top, bottom = call(
        functools.partial(join_body, bands),
        "join",
        (shape((bands, share, 10 * block), F32), shape((2, 4, wide, lanes), BF), edge, edge),
        [VMEM],
        [pltpu.VMEM((8 * sources, 128), F32), pltpu.VMEM((wide, 128), F32)],
    )(got)
    above = lax.ppermute(bottom, "row", down)
    below = lax.ppermute(top, "row", up)
    partial = lax.all_to_all(partial, "row", 0, 0)
    partial, above, below = lax.optimization_barrier((partial, above, below))
    scaling = 1.0 / math.sqrt(here * sources * band_rows * bands * wide)
    partial = call(
        functools.partial(sum_body, scaling), "sum", shape((sources, share, 10 * block), F32), [VMEM], []
    )(partial)
    grad_frames = call(
        back_body,
        "back",
        shape(frames_in.shape, BF),
        [VMEM] * 6,
        [
            pltpu.VMEM((wide + 2 * PAD, lanes), F32),
            pltpu.VMEM((3, 2, 6, wide, lanes), BF),
        ],
        flops=2 * cells * lanes * lanes * 9,
        moved=2 << 20,
    )(drive, above, below, kernel, cotangent, feedthrough.reshape(1, lanes))
    whole = lax.all_to_all(partial, "tm", 0, 0)
    grad_kernel, grad_readout = call(
        last_body, "last", (shape((9, block, lanes), F32), shape((block, lanes), F32)), [VMEM], []
    )(whole)
    return grad_frames, grad_kernel, grad_readout.T


def solution(mesh):
    placed = (
        P("tm", "row", None, None),
        P("tm", "row", None, None),
        P(),
        P(),
        P(),
        P("tm", None),
        P("row", None, None),
    )
    return jax.shard_map(
        local,
        mesh=mesh,
        in_specs=placed,
        out_specs=(P("tm", "row", None, None), P(None, "row", None), P(None, "row")),
        check_vma=False,
    )
```

```python
import functools
import math

import jax
import jax.numpy as jnp
from jax import lax
from jax.experimental import pallas as pl
from jax.experimental.pallas import tpu as pltpu
from jax.sharding import PartitionSpec as P

SQRT_TWO_PI = 0.7978845608
CUBIC = 0.044715
BF = jnp.bfloat16
F32 = jnp.float32
PAD = 8
CELLS = ((0, 0), (0, 1), (2, 0), (2, 1), (1, 0), (1, 1), (3, 0), (3, 1))
VMEM = pl.BlockSpec(memory_space=pltpu.VMEM)
HBM = pl.BlockSpec(memory_space=pltpu.MemorySpace.HBM)


def call(body, name, outs, ins, scratch, flops=1 << 20, moved=1 << 20, grant=40 << 20):
    many = isinstance(outs, (list, tuple))
    return pl.pallas_call(
        body,
        name=name,
        out_shape=outs,
        in_specs=ins,
        out_specs=[VMEM] * len(outs) if many else VMEM,
        scratch_shapes=scratch,
        cost_estimate=pl.CostEstimate(flops=flops, bytes_accessed=moved, transcendentals=0),
        compiler_params=pltpu.CompilerParams(vmem_limit_bytes=grant),
    )


def split3(value):
    high = value.astype(BF).astype(F32)
    rest = value - high
    middle = rest.astype(BF).astype(F32)
    return high, middle, rest - middle


def sublane(shape):
    return lax.broadcasted_iota(jnp.int32, shape, len(shape) - 2)


def gelu_slope(mixture):
    inside = SQRT_TWO_PI * (mixture + CUBIC * mixture * mixture * mixture)
    tangent = jnp.tanh(inside)
    return 0.5 * (1.0 + tangent) + 0.5 * mixture * (1.0 - tangent * tangent) * SQRT_TWO_PI * (
        1.0 + 3.0 * CUBIC * mixture * mixture
    )


def spread_body(frames, cotangent, decay, out, grid, slopes, rows, given, rates, parts, sems):
    wide, lanes = frames.shape[2:]
    copies = (
        pltpu.make_async_copy(frames, rows, sems.at[0]),
        pltpu.make_async_copy(cotangent, given, sems.at[1]),
        pltpu.make_async_copy(decay, rates, sems.at[2]),
    )
    for copy in copies:
        copy.start()
    for f in range(2):
        for row in range(4):
            grid[f, row, 0:PAD, :] = jnp.zeros((PAD, lanes), F32)
            grid[f, row, PAD + wide :, :] = jnp.zeros((PAD, lanes), F32)
    for copy in copies:
        copy.wait()
    for f in range(2):
        for row in range(4):
            grid[f, row, PAD : PAD + wide, :] = rows[f, row].astype(F32)
            slopes[f, row, PAD : PAD + wide, :] = given[f, row].astype(F32)
    for place, piece in enumerate(split3(rates[...])):
        parts[2 * place : 2 * place + 2, :] = piece
    parts[6:8, :] = jnp.zeros((2, lanes), F32)
    pieces = parts[...].astype(BF)
    step = sublane((8, lanes))
    for target in range(wide // 2):
        first = PAD + 2 * target
        for row in range(4):
            start = first - 1
            block = jnp.where(
                step < 4, grid[0, row, start : start + 8, :], grid[1, row, start - 4 : start + 4, :]
            )
            out[target, 8 * row : 8 * row + 8, :] = block.astype(BF)
        for f in range(2):
            block = slopes[f, 0, first : first + 8, :]
            for place, row in ((2, 2), (4, 1), (6, 3)):
                block = jnp.where(step < place, block, slopes[f, row, first - place : first - place + 8, :])
            out[target, 32 + 8 * f : 40 + 8 * f, :] = block.astype(BF)
        out[target, 48:56, :] = pieces


def cell_body(
    got,
    above,
    below,
    kernel,
    readout,
    start,
    out,
    grid,
    decay,
    gain,
    taps,
    driven,
    states,
    slopes,
    drive,
    turned,
    starts,
    sem,
):
    sources = got.shape[0]
    count = sources * 16
    lanes = got.shape[2]
    step = sublane((8, lanes))
    near = (step % 4) < 2
    mine = lax.axis_index("tm")
    fetch = pltpu.make_async_copy(start.at[:, pl.ds(pl.multiple_of(8 * (mine // 4), 8), 8)], starts, sem)
    fetch.start()

    def unpack(source, _):
        groups = [above[source], got[source, 0:8, :], got[source, 8:16, :]]
        groups += [got[source, 16:24, :], got[source, 24:32, :], below[source]]
        groups = [group.astype(F32) for group in groups]
        for pair in range(3):
            first, second = groups[2 * pair : 2 * pair + 2]
            rows = slice(8 * pair, 8 * pair + 8)
            grid[2 * source, rows, :] = jnp.where(step < 4, first, pltpu.roll(second, 4, 0))
            grid[2 * source + 1, rows, :] = jnp.where(step < 4, pltpu.roll(first, 4, 0), second)
        piece = got[source, 48:56, :].astype(F32)
        rate = piece + pltpu.roll(piece, 6, 0) + pltpu.roll(piece, 4, 0)
        decay[source] = rate
        gain[source] = jnp.sqrt(1.0 - rate * rate)
        return _

    lax.fori_loop(0, sources, unpack, 0, unroll=4)

    def gather(source, _):
        rows = pl.ds(pl.multiple_of(16 * source, 16), 16)
        for i in range(3):
            for j in range(3):
                place = 4 * i + j
                pair = []
                for f in range(2):
                    value = jnp.where(
                        near,
                        grid[2 * source + f, place : place + 8, :],
                        grid[2 * source + f, place + 6 : place + 14, :],
                    )
                    pair.append(value)
                tap = 3 * i + j
                taps[rows, lanes * tap : lanes * tap + lanes] = jnp.concatenate(pair, axis=0).astype(BF)
        return _

    lax.fori_loop(0, sources, gather, 0, unroll=2)

    chunk = min(count, 256)

    def convolve(part, _):
        rows = pl.ds(pl.multiple_of(part * chunk, chunk), chunk)
        driven[rows, :] = jnp.dot(taps[rows, :], kernel[...], preferred_element_type=F32)
        return _

    lax.fori_loop(0, count // chunk, convolve, 0)

    fetch.wait()
    offset = 2 * (mine % 4)
    begin = pltpu.roll(starts[0], (8 - offset) % 8, 0)
    for place, row in ((2, 2), (4, 1), (6, 3)):
        begin = jnp.where(step < place, begin, pltpu.roll(starts[row], (8 + place - offset) % 8, 0))

    def advance(source, state):
        pair = []
        for f in range(2):
            rate = jnp.broadcast_to(decay[source, f : f + 1, :], state.shape)
            size = jnp.broadcast_to(gain[source, f : f + 1, :], state.shape)
            now = driven[pl.ds(pl.multiple_of(16 * source + 8 * f, 8), 8), :]
            state = rate * state + size * now
            pair.append(state)
        states[pl.ds(pl.multiple_of(16 * source, 16), 16), :] = jnp.concatenate(pair, axis=0).astype(BF)
        return state

    lax.fori_loop(0, sources, advance, begin, unroll=4)

    def mix(part, _):
        rows = pl.ds(pl.multiple_of(part * 64, 64), 64)
        mixture = jnp.dot(states[rows, :], readout[...], preferred_element_type=F32)
        upstream = jnp.concatenate(
            [
                got[4 * part + source, 32 + 8 * f : 40 + 8 * f, :].astype(F32)
                for source in range(4)
                for f in range(2)
            ],
            axis=0,
        )
        slope = (upstream * gelu_slope(mixture)).astype(BF)
        slopes[rows, :] = slope
        driven[rows, :] = lax.dot_general(
            slope, readout[...], (((1,), (1,)), ((), ())), preferred_element_type=F32
        )
        return _

    lax.fori_loop(0, count // 64, mix, 0, unroll=2)

    def retreat(turn, carried):
        adjoint, later = carried
        source = sources - 1 - turn
        pair = []
        for f in (1, 0):
            now = driven[pl.ds(pl.multiple_of(16 * source + 8 * f, 8), 8), :]
            adjoint = now + later * adjoint
            later = jnp.broadcast_to(decay[source, f : f + 1, :], adjoint.shape)
            value = jnp.broadcast_to(gain[source, f : f + 1, :], adjoint.shape) * adjoint
            pair.append(value)
            out[source, 0:8, 10 * lanes + f * lanes : 11 * lanes + f * lanes] = value.astype(BF)
        drive[pl.ds(pl.multiple_of(16 * source, 16), 16), :] = jnp.concatenate(pair[::-1], axis=0)
        return adjoint, later

    nothing = jnp.zeros((8, lanes), F32)
    lax.fori_loop(0, sources, retreat, (nothing, nothing), unroll=4)

    turned[...] = drive[...].astype(BF).T
    share = lanes // sources
    for tap in range(9):
        term = jnp.dot(turned[...], taps[:, lanes * tap : lanes * tap + lanes], preferred_element_type=F32)
        out[:, :, lanes * tap : lanes * tap + lanes] = term.astype(BF).reshape(sources, share, lanes)
    term = jnp.dot(states[...].T, slopes[...], preferred_element_type=F32)
    out[:, :, 9 * lanes : 10 * lanes] = term.astype(BF).reshape(sources, share, lanes)


def join_body(bands, got, total, frames, top, bottom, cells, grid):
    sources, share, width = got.shape
    lanes = width // 12

    def add(source, carried):
        return carried + got[source, :, : 10 * lanes].astype(F32)

    sums = lax.fori_loop(0, sources, add, jnp.zeros((share, 10 * lanes), F32), unroll=2)
    block = lanes // bands
    for band in range(bands):
        total[band] = jnp.concatenate(
            [sums[:, lanes * k + block * band : lanes * k + block * band + block] for k in range(10)], axis=1
        ).astype(BF)

    for f in range(2):
        for part in range(lanes // 128):
            for source in range(sources):
                first = (10 + f) * lanes + 128 * part
                cells[8 * source : 8 * source + 8, :] = got[source, 0:8, first : first + 128].astype(F32)
            for place, (row, column) in enumerate(CELLS):
                grid[pl.ds(column, sources, stride=2), :] = cells[pl.ds(place, sources, stride=8), :]
                if column == 1:
                    value = grid[...].astype(BF)
                    frames[f, row, :, 128 * part : 128 * part + 128] = value
                    if row == 0:
                        top[f, :, 128 * part : 128 * part + 128] = value
                    if row == 3:
                        bottom[f, :, 128 * part : 128 * part + 128] = value


def back_body(drive, above, below, kernel, cotangent, feedthrough, out, grid, moved):
    wide = drive.shape[2]
    lanes = drive.shape[3]
    for row in range(6):
        for f in range(2):
            if row == 0:
                source = above[f]
            elif row == 5:
                source = below[f]
            else:
                source = drive[f, row - 1]
            grid[0:PAD, :] = jnp.zeros((PAD, lanes), F32)
            grid[PAD + wide :, :] = jnp.zeros((PAD, lanes), F32)
            grid[PAD : PAD + wide, :] = source.astype(F32)
            for shift in range(3):
                moved[shift, f, row] = grid[PAD - 1 + shift : PAD - 1 + shift + wide, :].astype(BF)
    for f in range(2):
        for half in range(2):
            total = jnp.zeros((2 * wide, lanes), F32)
            for i in range(3):
                for j in range(3):
                    first = 2 - i + 2 * half
                    cells = moved[2 - j, f, first : first + 2].reshape(2 * wide, lanes)
                    total = total + lax.dot_general(
                        cells, kernel[3 * i + j], (((1,), (1,)), ((), ())), preferred_element_type=F32
                    )
            total = total.reshape(2, wide, lanes)
            for row in range(2):
                place = 2 * half + row
                out[f, place] = (total[row] + feedthrough[...] * cotangent[f, place].astype(F32)).astype(BF)


def sum_body(scaling, got, out):
    total = got[0].astype(F32)
    for band in range(1, got.shape[0]):
        total = total + got[band].astype(F32)
    total = (total * scaling).astype(BF)
    for target in range(out.shape[0]):
        out[target] = total


def last_body(got, kernel_out, readout_out):
    sources, share, width = got.shape
    turned = got[...].astype(F32).reshape(sources * share, width).T
    block = width // 10
    for k in range(9):
        kernel_out[k] = turned[block * k : block * k + block]
    readout_out[...] = turned[9 * block :]


def local(frames_in, cotangent, kernel, readout, feedthrough, decay_rate, start_state):
    here, band_rows, wide, lanes = frames_in.shape
    sources, bands = lax.axis_size("tm"), lax.axis_size("row")
    cells = sources * 16
    share = lanes // sources
    block = lanes // bands
    shape = jax.ShapeDtypeStruct
    down = [(i, i + 1) for i in range(bands - 1)]
    up = [(i + 1, i) for i in range(bands - 1)]

    send = call(
        spread_body,
        "spread",
        shape((sources, 56, lanes), BF),
        [HBM] * 3,
        [
            pltpu.VMEM((2, 4, wide + 2 * PAD, lanes), F32),
            pltpu.VMEM((2, 4, wide + 2 * PAD, lanes), F32),
            pltpu.VMEM((2, 4, wide, lanes), BF),
            pltpu.VMEM((2, 4, wide, lanes), BF),
            pltpu.VMEM((2, lanes), F32),
            pltpu.VMEM((8, lanes), F32),
            pltpu.SemaphoreType.DMA((3,)),
        ],
        grant=63 << 20,
    )(frames_in, cotangent, decay_rate)
    got = lax.all_to_all(send, "tm", 0, 0)
    above = lax.ppermute(got[:, 24:32], "row", down)
    below = lax.ppermute(got[:, 0:8], "row", up)
    send = call(
        cell_body,
        "cells",
        shape((sources, max(8, share), 12 * lanes), BF),
        [VMEM] * 5 + [HBM],
        [
            pltpu.VMEM((2 * sources, 24, lanes), F32),
            pltpu.VMEM((sources, 8, lanes), F32),
            pltpu.VMEM((sources, 8, lanes), F32),
            pltpu.VMEM((cells, 9 * lanes), BF),
            pltpu.VMEM((cells, lanes), F32),
            pltpu.VMEM((cells, lanes), BF),
            pltpu.VMEM((cells, lanes), BF),
            pltpu.VMEM((cells, lanes), F32),
            pltpu.VMEM((lanes, cells), BF),
            pltpu.VMEM((4, 8, lanes), F32),
            pltpu.SemaphoreType.DMA,
        ],
        flops=2 * cells * lanes * lanes * 21,
        moved=4 << 20,
    )(got, above, below, kernel.reshape(9 * lanes, lanes), readout, start_state)
    got = lax.all_to_all(send, "tm", 0, 0)
    edge = shape((2, wide, lanes), BF)
    partial, drive, top, bottom = call(
        functools.partial(join_body, bands),
        "join",
        (shape((bands, share, 10 * block), BF), shape((2, 4, wide, lanes), BF), edge, edge),
        [VMEM],
        [pltpu.VMEM((8 * sources, 128), F32), pltpu.VMEM((wide, 128), F32)],
    )(got)
    above = lax.ppermute(bottom, "row", down)
    below = lax.ppermute(top, "row", up)
    partial = lax.all_to_all(partial, "row", 0, 0)
    scaling = 1.0 / math.sqrt(here * sources * band_rows * bands * wide)
    partial = call(
        functools.partial(sum_body, scaling), "sum", shape((sources, share, 10 * block), BF), [VMEM], []
    )(partial)
    grad_frames = call(
        back_body,
        "back",
        shape(frames_in.shape, BF),
        [VMEM] * 6,
        [
            pltpu.VMEM((wide + 2 * PAD, lanes), F32),
            pltpu.VMEM((3, 2, 6, wide, lanes), BF),
        ],
        flops=2 * cells * lanes * lanes * 9,
        moved=2 << 20,
    )(drive, above, below, kernel, cotangent, feedthrough.reshape(1, lanes))
    whole = lax.all_to_all(partial, "tm", 0, 0)
    grad_kernel, grad_readout = call(
        last_body, "last", (shape((9, block, lanes), F32), shape((block, lanes), F32)), [VMEM], []
    )(whole)
    return grad_frames, grad_kernel, grad_readout.T


def solution(mesh):
    placed = (
        P("tm", "row", None, None),
        P("tm", "row", None, None),
        P(),
        P(),
        P(),
        P("tm", None),
        P("row", None, None),
    )
    return jax.shard_map(
        local,
        mesh=mesh,
        in_specs=placed,
        out_specs=(P("tm", "row", None, None), P(None, "row", None), P(None, "row")),
        check_vma=False,
    )
```

```python
import functools
import math

import jax
import jax.numpy as jnp
from jax import lax
from jax.experimental import pallas as pl
from jax.experimental.pallas import tpu as pltpu
from jax.sharding import PartitionSpec as P

SQRT_TWO_PI = 0.7978845608
CUBIC = 0.044715
BF = jnp.bfloat16
F32 = jnp.float32
PAD = 8
CELLS = ((0, 0), (0, 1), (2, 0), (2, 1), (1, 0), (1, 1), (3, 0), (3, 1))
VMEM = pl.BlockSpec(memory_space=pltpu.VMEM)
HBM = pl.BlockSpec(memory_space=pltpu.MemorySpace.HBM)


def call(body, name, outs, ins, scratch, flops=1 << 20, moved=1 << 20, grant=40 << 20, to=None, alias=None):
    many = isinstance(outs, (list, tuple))
    return pl.pallas_call(
        body,
        name=name,
        out_shape=outs,
        in_specs=ins,
        out_specs=[VMEM] * len(outs) if many else (to or VMEM),
        input_output_aliases=alias or {},
        scratch_shapes=scratch,
        cost_estimate=pl.CostEstimate(flops=flops, bytes_accessed=moved, transcendentals=0),
        compiler_params=pltpu.CompilerParams(vmem_limit_bytes=grant),
    )


def split3(value):
    high = value.astype(BF).astype(F32)
    rest = value - high
    middle = rest.astype(BF).astype(F32)
    return high, middle, rest - middle


def sublane(shape):
    return lax.broadcasted_iota(jnp.int32, shape, len(shape) - 2)


def gelu_slope(mixture):
    inside = SQRT_TWO_PI * (mixture + CUBIC * mixture * mixture * mixture)
    tangent = jnp.tanh(inside)
    return 0.5 * (1.0 + tangent) + 0.5 * mixture * (1.0 - tangent * tangent) * SQRT_TWO_PI * (
        1.0 + 3.0 * CUBIC * mixture * mixture
    )


def halo_body(frames, cotangent, start, out, begin, rows, slopes, starts, sems):
    wide = frames.shape[2]
    mine = lax.axis_index("tm")
    group = pl.multiple_of(8 * (mine // 4), 8)
    copies = (
        pltpu.make_async_copy(start.at[:, pl.ds(group, 8)], starts, sems.at[0]),
        pltpu.make_async_copy(frames.at[:, 2:4], rows, sems.at[1]),
        pltpu.make_async_copy(cotangent.at[:, 3], slopes, sems.at[2]),
    )
    for copy in copies:
        copy.start()
    for copy in copies:
        copy.wait()
    for f in range(2):
        for row in range(2):
            out[pl.ds((2 * f + row) * wide, wide), :] = rows[f, row]
        out[pl.ds((4 + f) * wide, wide), :] = slopes[f]
    offset = 2 * (mine % 4)
    step = sublane(begin.shape)
    total = jnp.zeros(begin.shape, F32)
    for place, row in ((2, 1), (4, 0), (6, 2)):
        moved = pltpu.roll(starts[row], (8 + place - offset) % 8, 0)
        total = jnp.where((step >= place) & (step < place + 2), moved, total)
    begin[...] = total
    pieces = split3(pltpu.roll(starts[3], (8 - offset) % 8, 0))
    total = jnp.where(step < 2, pieces[0], 0.0)
    total = jnp.where((step >= 2) & (step < 4), pltpu.roll(pieces[1], 2, 0), total)
    total = jnp.where((step >= 4) & (step < 6), pltpu.roll(pieces[2], 4, 0), total)
    out[pl.ds(6 * wide, 8), :] = total.astype(BF)


def own_body(frames, cotangent, decay, out, pieces, grid, slopes, rows, given, rates, parts, sems):
    wide, lanes = frames.shape[2:]
    copies = (
        pltpu.make_async_copy(frames, rows, sems.at[0]),
        pltpu.make_async_copy(cotangent, given, sems.at[1]),
        pltpu.make_async_copy(decay, rates, sems.at[2]),
    )
    for copy in copies:
        copy.start()
    for f in range(2):
        for row in range(4):
            grid[f, row, 0:PAD, :] = jnp.zeros((PAD, lanes), F32)
            grid[f, row, PAD + wide :, :] = jnp.zeros((PAD, lanes), F32)
    for copy in copies:
        copy.wait()
    for f in range(2):
        for row in range(4):
            grid[f, row, PAD : PAD + wide, :] = rows[f, row].astype(F32)
        for row in range(3):
            slopes[f, row, PAD : PAD + wide, :] = given[f, row].astype(F32)
    for place, piece in enumerate(split3(rates[...])):
        parts[2 * place : 2 * place + 2, :] = piece
    parts[6:8, :] = jnp.zeros((2, lanes), F32)
    pieces[...] = parts[...].astype(BF)
    step = sublane((8, lanes))
    for target in range(wide // 2):
        first = PAD + 2 * target
        for f in range(2):
            for pair in range(2):
                start = first - 1
                block = jnp.where(
                    step < 4,
                    grid[f, 2 * pair, start : start + 8, :],
                    grid[f, 2 * pair + 1, start - 4 : start + 4, :],
                )
                out[target, 16 * f + 8 * pair : 16 * f + 8 * pair + 8, :] = block.astype(BF)
            block = slopes[f, 1, first - 2 : first + 6, :]
            for place, row in ((4, 0), (6, 2)):
                block = jnp.where(step < place, block, slopes[f, row, first - place : first - place + 8, :])
            out[target, 32 + 8 * f : 40 + 8 * f, :] = block.astype(BF)


def spread_body(own, pieces, halo, out, grid, slopes):
    wide = (halo.shape[0] - 8) // 6
    lanes = halo.shape[1]
    for f in range(2):
        for row in range(2):
            grid[f, row, 0:PAD, :] = jnp.zeros((PAD, lanes), F32)
            grid[f, row, PAD + wide :, :] = jnp.zeros((PAD, lanes), F32)
            grid[f, row, PAD : PAD + wide, :] = halo[pl.ds((2 * f + row) * wide, wide), :].astype(F32)
        slopes[f, PAD : PAD + wide, :] = halo[pl.ds((4 + f) * wide, wide), :].astype(F32)
    step = sublane((8, lanes))
    for target in range(wide // 2):
        first = PAD + 2 * target
        for f in range(2):
            start = first - 1
            block = jnp.where(step < 4, grid[f, 0, start : start + 8, :], grid[f, 1, start - 4 : start + 4, :])
            out[target, 32 * f : 32 * f + 8, :] = block.astype(BF)
            out[target, 32 * f + 8 : 32 * f + 24, :] = own[target, 16 * f : 16 * f + 16, :]
            block = own[target, 32 + 8 * f : 40 + 8 * f, :].astype(F32)
            block = jnp.where(step < 2, slopes[f, first : first + 8, :], block)
            out[target, 32 * f + 24 : 32 * f + 32, :] = block.astype(BF)
        out[target, 64:72, :] = pieces[...]


def cell_body(
    got, kernel, readout, start, halo, out, grid, decay, gain, taps, driven, states, slopes, drive, turned
):
    sources = got.shape[0]
    count = sources * 16
    wide = (halo.shape[0] - 8) // 6
    lanes = got.shape[2]
    step = sublane((8, lanes))
    is_first = lax.axis_index("row") == 0
    low = jnp.where(is_first & (step < 2), 0.0, 1.0)
    high = jnp.where(is_first & (step >= 4) & (step < 6), 0.0, 1.0)
    near = (step % 4) < 2

    def unpack(source, _):
        for f in range(2):
            grid[2 * source + f] = got[source, 32 * f : 32 * f + 24, :].astype(F32)
        piece = got[source, 64:72, :].astype(F32)
        rate = piece + pltpu.roll(piece, 6, 0) + pltpu.roll(piece, 4, 0)
        decay[source] = rate
        gain[source] = jnp.sqrt(1.0 - rate * rate)
        return _

    lax.fori_loop(0, sources, unpack, 0, unroll=4)

    def gather(source, _):
        rows = pl.ds(pl.multiple_of(16 * source, 16), 16)
        for i in range(3):
            for j in range(3):
                place = 4 * i + j
                pair = []
                for f in range(2):
                    value = jnp.where(
                        near,
                        grid[2 * source + f, place : place + 8, :],
                        grid[2 * source + f, place + 6 : place + 14, :],
                    )
                    if i == 2:
                        value = value * low
                    if i == 0:
                        value = value * high
                    pair.append(value)
                tap = 3 * i + j
                taps[rows, lanes * tap : lanes * tap + lanes] = jnp.concatenate(pair, axis=0).astype(BF)
        return _

    lax.fori_loop(0, sources, gather, 0, unroll=2)

    chunk = min(count, 256)

    def convolve(part, _):
        rows = pl.ds(pl.multiple_of(part * chunk, chunk), chunk)
        driven[rows, :] = jnp.dot(taps[rows, :], kernel[...], preferred_element_type=F32)
        return _

    lax.fori_loop(0, count // chunk, convolve, 0)

    tail = halo[6 * wide : 6 * wide + 8, :].astype(F32)
    tail = tail + pltpu.roll(tail, 6, 0) + pltpu.roll(tail, 4, 0)
    begin = jnp.where(step < 2, tail, start[...])

    def advance(source, state):
        pair = []
        for f in range(2):
            rate = jnp.broadcast_to(decay[source, f : f + 1, :], state.shape)
            size = jnp.broadcast_to(gain[source, f : f + 1, :], state.shape)
            now = driven[pl.ds(pl.multiple_of(16 * source + 8 * f, 8), 8), :]
            state = rate * state + size * now
            pair.append(state)
        states[pl.ds(pl.multiple_of(16 * source, 16), 16), :] = jnp.concatenate(pair, axis=0).astype(BF)
        return state

    lax.fori_loop(0, sources, advance, begin, unroll=4)

    def mix(part, _):
        rows = pl.ds(pl.multiple_of(part * 64, 64), 64)
        mixture = jnp.dot(states[rows, :], readout[...], preferred_element_type=F32)
        upstream = jnp.concatenate(
            [
                got[4 * part + source, 32 * f + 24 : 32 * f + 32, :].astype(F32)
                for source in range(4)
                for f in range(2)
            ],
            axis=0,
        )
        slope = (upstream * gelu_slope(mixture)).astype(BF)
        slopes[rows, :] = slope
        driven[rows, :] = lax.dot_general(
            slope, readout[...], (((1,), (1,)), ((), ())), preferred_element_type=F32
        )
        return _

    lax.fori_loop(0, count // 64, mix, 0, unroll=4)

    def retreat(turn, carried):
        adjoint, later = carried
        source = sources - 1 - turn
        pair = []
        for f in (1, 0):
            now = driven[pl.ds(pl.multiple_of(16 * source + 8 * f, 8), 8), :]
            adjoint = now + later * adjoint
            later = jnp.broadcast_to(decay[source, f : f + 1, :], adjoint.shape)
            value = jnp.broadcast_to(gain[source, f : f + 1, :], adjoint.shape) * adjoint
            pair.append(value)
            out[source, 0:8, 10 * lanes + f * lanes : 11 * lanes + f * lanes] = value.astype(BF)
        drive[pl.ds(pl.multiple_of(16 * source, 16), 16), :] = jnp.concatenate(pair[::-1], axis=0)
        return adjoint, later

    nothing = jnp.zeros((8, lanes), F32)
    lax.fori_loop(0, sources, retreat, (nothing, nothing), unroll=4)

    turned[...] = drive[...].astype(BF).T
    share = lanes // sources
    for tap in range(9):
        term = jnp.dot(turned[...], taps[:, lanes * tap : lanes * tap + lanes], preferred_element_type=F32)
        out[:, :, lanes * tap : lanes * tap + lanes] = term.astype(BF).reshape(sources, share, lanes)
    term = jnp.dot(states[...].T, slopes[...], preferred_element_type=F32)
    out[:, :, 9 * lanes : 10 * lanes] = term.astype(BF).reshape(sources, share, lanes)


def join_body(bands, got, total, frames, top, cells, grid):
    sources, share, width = got.shape
    lanes = width // 12

    def add(source, carried):
        return carried + got[source, :, : 10 * lanes].astype(F32)

    sums = lax.fori_loop(0, sources, add, jnp.zeros((share, 10 * lanes), F32), unroll=2)
    block = lanes // bands
    for band in range(bands):
        total[band] = jnp.concatenate(
            [sums[:, lanes * k + block * band : lanes * k + block * band + block] for k in range(10)], axis=1
        ).astype(BF)

    for f in range(2):
        for part in range(lanes // 128):
            for source in range(sources):
                first = (10 + f) * lanes + 128 * part
                cells[8 * source : 8 * source + 8, :] = got[source, 0:8, first : first + 128].astype(F32)
            for place, (row, column) in enumerate(CELLS):
                grid[pl.ds(column, sources, stride=2), :] = cells[pl.ds(place, sources, stride=8), :]
                if column == 1:
                    value = grid[...].astype(BF)
                    frames[f, row, :, 128 * part : 128 * part + 128] = value
                    if row < 2:
                        top[f, row, :, 128 * part : 128 * part + 128] = value


def back_body(first, bands, *refs):
    if first:
        drive, below, kernel, cotangent, feedthrough, _, out, grid, moved, done, sem = refs
    else:
        drive, kernel, cotangent, feedthrough, out, grid, moved, done, sem = refs
    wide, lanes = drive.shape[2:]
    band = lax.axis_index("row")
    for row in range(first, first + 4):
        keep = None
        if row == 0:
            keep = jnp.where(band == 0, 0.0, 1.0)
        if row == 5:
            keep = jnp.where(band == bands - 1, 0.0, 1.0)
        for f in range(2):
            source = (drive[f, row] if row < 4 else below[f, row - 4]).astype(F32)
            if keep is not None:
                source = source * keep
            grid[f, row - first, 0:PAD, :] = jnp.zeros((PAD, lanes), F32)
            grid[f, row - first, PAD + wide :, :] = jnp.zeros((PAD, lanes), F32)
            grid[f, row - first, PAD : PAD + wide, :] = source
            for shift in range(3):
                begin = PAD - 1 + shift
                moved[shift, f, row - first] = grid[f, row - first, begin : begin + wide, :].astype(BF)
    for f in range(2):
        total = jnp.zeros((2 * wide, lanes), F32)
        for i in range(3):
            for j in range(3):
                cells = moved[2 - j, f, 2 - i : 4 - i].reshape(2 * wide, lanes)
                total = total + lax.dot_general(
                    cells, kernel[3 * i + j], (((1,), (1,)), ((), ())), preferred_element_type=F32
                )
        given = cotangent[f, first : first + 2].astype(F32).reshape(2 * wide, lanes)
        done[f] = (total + feedthrough[...] * given).astype(BF).reshape(2, wide, lanes)
    store = pltpu.make_async_copy(done, out.at[:, first : first + 2], sem)
    store.start()
    store.wait()


def sum_body(scaling, got, out):
    total = got[0].astype(F32)
    for band in range(1, got.shape[0]):
        total = total + got[band].astype(F32)
    total = (total * scaling).astype(BF)
    for target in range(out.shape[0]):
        out[target] = total


def last_body(got, kernel_out, readout_out):
    sources, share, width = got.shape
    turned = got[...].astype(F32).reshape(sources * share, width).T
    block = width // 10
    for k in range(9):
        kernel_out[k] = turned[block * k : block * k + block]
    readout_out[...] = turned[9 * block :]


def local(frames_in, cotangent, kernel, readout, feedthrough, decay_rate, start_state):
    here, band_rows, wide, lanes = frames_in.shape
    sources, bands = lax.axis_size("tm"), lax.axis_size("row")
    cells = sources * 16
    share = lanes // sources
    block = lanes // bands
    shape = jax.ShapeDtypeStruct
    down = [(i, (i + 1) % bands) for i in range(bands)]
    up = [((i + 1) % bands, i) for i in range(bands)]

    edge, begin = call(
        halo_body,
        "halo",
        (shape((6 * wide + 8, lanes), BF), shape((8, lanes), F32)),
        [HBM] * 3,
        [
            pltpu.VMEM((2, 2, wide, lanes), BF),
            pltpu.VMEM((2, wide, lanes), BF),
            pltpu.VMEM((4, 8, lanes), F32),
            pltpu.SemaphoreType.DMA((3,)),
        ],
        grant=63 << 20,
    )(frames_in, cotangent, start_state)
    edge = lax.ppermute(edge, "row", down)
    own, pieces = call(
        own_body,
        "own",
        (shape((sources, 48, lanes), BF), shape((8, lanes), BF)),
        [HBM] * 3,
        [
            pltpu.VMEM((2, 4, wide + 2 * PAD, lanes), F32),
            pltpu.VMEM((2, 3, wide + 2 * PAD, lanes), F32),
            pltpu.VMEM((2, 4, wide, lanes), BF),
            pltpu.VMEM((2, 4, wide, lanes), BF),
            pltpu.VMEM((2, lanes), F32),
            pltpu.VMEM((8, lanes), F32),
            pltpu.SemaphoreType.DMA((3,)),
        ],
        moved=8 << 20,
    )(frames_in, cotangent, decay_rate)
    send = call(
        spread_body,
        "spread",
        shape((sources, 72, lanes), BF),
        [VMEM] * 3,
        [
            pltpu.VMEM((2, 2, wide + 2 * PAD, lanes), F32),
            pltpu.VMEM((2, wide + 2 * PAD, lanes), F32),
        ],
    )(own, pieces, edge)
    got = lax.all_to_all(send, "tm", 0, 0)
    send = call(
        cell_body,
        "cells",
        shape((sources, max(8, share), 12 * lanes), BF),
        [VMEM] * 5,
        [
            pltpu.VMEM((2 * sources, 24, lanes), F32),
            pltpu.VMEM((sources, 8, lanes), F32),
            pltpu.VMEM((sources, 8, lanes), F32),
            pltpu.VMEM((cells, 9 * lanes), BF),
            pltpu.VMEM((cells, lanes), F32),
            pltpu.VMEM((cells, lanes), BF),
            pltpu.VMEM((cells, lanes), BF),
            pltpu.VMEM((cells, lanes), F32),
            pltpu.VMEM((lanes, cells), BF),
        ],
        flops=2 * cells * lanes * lanes * 21,
        moved=4 << 20,
    )(got, kernel.reshape(9 * lanes, lanes), readout, begin, edge)
    got = lax.all_to_all(send, "tm", 0, 0)
    partial, drive, top = call(
        functools.partial(join_body, bands),
        "join",
        (
            shape((bands, share, 10 * block), BF),
            shape((2, 4, wide, lanes), BF),
            shape((2, 2, wide, lanes), BF),
        ),
        [VMEM],
        [pltpu.VMEM((8 * sources, 128), F32), pltpu.VMEM((wide, 128), F32)],
    )(got)
    below = lax.ppermute(top, "row", up)
    partial = lax.all_to_all(partial, "row", 0, 0)
    scaling = 1.0 / math.sqrt(here * sources * band_rows * bands * wide)
    partial = call(
        functools.partial(sum_body, scaling), "sum", shape((sources, share, 10 * block), BF), [VMEM], []
    )(partial)

    def back(first, ins, **more):
        return call(
            functools.partial(back_body, first, bands),
            "back",
            shape(frames_in.shape, BF),
            ins,
            [
                pltpu.VMEM((2, 4, wide + 2 * PAD, lanes), F32),
                pltpu.VMEM((3, 2, 4, wide, lanes), BF),
                pltpu.VMEM((2, 2, wide, lanes), BF),
                pltpu.SemaphoreType.DMA,
            ],
            flops=cells * lanes * lanes * 9,
            moved=2 << 20,
            to=HBM,
            **more,
        )

    through = feedthrough.reshape(1, lanes)
    grad_frames = back(0, [VMEM] * 4)(drive, kernel, cotangent, through)
    grad_frames = back(2, [VMEM] * 5 + [HBM], alias={5: 0})(
        drive, below, kernel, cotangent, through, grad_frames
    )
    whole = lax.all_to_all(partial, "tm", 0, 0)
    grad_kernel, grad_readout = call(
        last_body, "last", (shape((9, block, lanes), F32), shape((block, lanes), F32)), [VMEM], []
    )(whole)
    return grad_frames, grad_kernel, grad_readout.T


def solution(mesh):
    placed = (
        P("tm", "row", None, None),
        P("tm", "row", None, None),
        P(),
        P(),
        P(),
        P("tm", None),
        P("row", None, None),
    )
    return jax.shard_map(
        local,
        mesh=mesh,
        in_specs=placed,
        out_specs=(P("tm", "row", None, None), P(None, "row", None), P(None, "row")),
        check_vma=False,
    )
```

```python
import functools
import math

import jax
import jax.numpy as jnp
from jax import lax
from jax.experimental import pallas as pl
from jax.experimental.pallas import tpu as pltpu
from jax.sharding import PartitionSpec as P

SQRT_TWO_PI = 0.7978845608
CUBIC = 0.044715
BF = jnp.bfloat16
F32 = jnp.float32
PAD = 8
CELLS = ((0, 0), (0, 1), (2, 0), (2, 1), (1, 0), (1, 1), (3, 0), (3, 1))
VMEM = pl.BlockSpec(memory_space=pltpu.VMEM)
HBM = pl.BlockSpec(memory_space=pltpu.MemorySpace.HBM)


def call(body, name, outs, ins, scratch, flops=1 << 20, moved=1 << 20, grant=40 << 20, to=None, alias=None):
    many = isinstance(outs, (list, tuple))
    return pl.pallas_call(
        body,
        name=name,
        out_shape=outs,
        in_specs=ins,
        out_specs=[VMEM] * len(outs) if many else (to or VMEM),
        input_output_aliases=alias or {},
        scratch_shapes=scratch,
        cost_estimate=pl.CostEstimate(flops=flops, bytes_accessed=moved, transcendentals=0),
        compiler_params=pltpu.CompilerParams(vmem_limit_bytes=grant),
    )


def split3(value):
    high = value.astype(BF).astype(F32)
    rest = value - high
    middle = rest.astype(BF).astype(F32)
    return high, middle, rest - middle


def sublane(shape):
    return lax.broadcasted_iota(jnp.int32, shape, len(shape) - 2)


def gelu_slope(mixture):
    inside = SQRT_TWO_PI * (mixture + CUBIC * mixture * mixture * mixture)
    tangent = jnp.tanh(inside)
    return 0.5 * (1.0 + tangent) + 0.5 * mixture * (1.0 - tangent * tangent) * SQRT_TWO_PI * (
        1.0 + 3.0 * CUBIC * mixture * mixture
    )


def halo_body(frames, cotangent, start, out, begin, rows, slopes, starts, sems):
    wide = frames.shape[2]
    mine = lax.axis_index("tm")
    group = pl.multiple_of(8 * (mine // 4), 8)
    copies = (
        pltpu.make_async_copy(start.at[:, pl.ds(group, 8)], starts, sems.at[0]),
        pltpu.make_async_copy(frames.at[:, 2:4], rows, sems.at[1]),
        pltpu.make_async_copy(cotangent.at[:, 3], slopes, sems.at[2]),
    )
    for copy in copies:
        copy.start()
    for copy in copies:
        copy.wait()
    for f in range(2):
        for row in range(2):
            out[pl.ds((2 * f + row) * wide, wide), :] = rows[f, row]
        out[pl.ds((4 + f) * wide, wide), :] = slopes[f]
    offset = 2 * (mine % 4)
    step = sublane(begin.shape)
    total = jnp.zeros(begin.shape, F32)
    for place, row in ((2, 1), (4, 0), (6, 2)):
        moved = pltpu.roll(starts[row], (8 + place - offset) % 8, 0)
        total = jnp.where((step >= place) & (step < place + 2), moved, total)
    begin[...] = total
    pieces = split3(pltpu.roll(starts[3], (8 - offset) % 8, 0))
    total = jnp.where(step < 2, pieces[0], 0.0)
    total = jnp.where((step >= 2) & (step < 4), pltpu.roll(pieces[1], 2, 0), total)
    total = jnp.where((step >= 4) & (step < 6), pltpu.roll(pieces[2], 4, 0), total)
    out[pl.ds(6 * wide, 8), :] = total.astype(BF)


def own_body(frames, cotangent, decay, out, pieces, grid, slopes, rows, given, rates, parts, sems):
    wide, lanes = frames.shape[2:]
    copies = (
        pltpu.make_async_copy(frames, rows, sems.at[0]),
        pltpu.make_async_copy(cotangent, given, sems.at[1]),
        pltpu.make_async_copy(decay, rates, sems.at[2]),
    )
    for copy in copies:
        copy.start()
    for f in range(2):
        for row in range(4):
            grid[f, row, 0:PAD, :] = jnp.zeros((PAD, lanes), F32)
            grid[f, row, PAD + wide :, :] = jnp.zeros((PAD, lanes), F32)
    for copy in copies:
        copy.wait()
    for f in range(2):
        for row in range(4):
            grid[f, row, PAD : PAD + wide, :] = rows[f, row].astype(F32)
        for row in range(3):
            slopes[f, row, PAD : PAD + wide, :] = given[f, row].astype(F32)
    for place, piece in enumerate(split3(rates[...])):
        parts[2 * place : 2 * place + 2, :] = piece
    parts[6:8, :] = jnp.zeros((2, lanes), F32)
    pieces[...] = parts[...].astype(BF)
    step = sublane((8, lanes))
    for target in range(wide // 2):
        first = PAD + 2 * target
        for f in range(2):
            for pair in range(2):
                start = first - 1
                block = jnp.where(
                    step < 4,
                    grid[f, 2 * pair, start : start + 8, :],
                    grid[f, 2 * pair + 1, start - 4 : start + 4, :],
                )
                out[target, 16 * f + 8 * pair : 16 * f + 8 * pair + 8, :] = block.astype(BF)
            block = slopes[f, 1, first - 2 : first + 6, :]
            for place, row in ((4, 0), (6, 2)):
                block = jnp.where(step < place, block, slopes[f, row, first - place : first - place + 8, :])
            out[target, 32 + 8 * f : 40 + 8 * f, :] = block.astype(BF)


def spread_body(own, pieces, halo, out, grid, slopes):
    wide = (halo.shape[0] - 8) // 6
    lanes = halo.shape[1]
    for f in range(2):
        for row in range(2):
            grid[f, row, 0:PAD, :] = jnp.zeros((PAD, lanes), F32)
            grid[f, row, PAD + wide :, :] = jnp.zeros((PAD, lanes), F32)
            grid[f, row, PAD : PAD + wide, :] = halo[pl.ds((2 * f + row) * wide, wide), :].astype(F32)
        slopes[f, PAD : PAD + wide, :] = halo[pl.ds((4 + f) * wide, wide), :].astype(F32)
    step = sublane((8, lanes))
    for target in range(wide // 2):
        first = PAD + 2 * target
        for f in range(2):
            start = first - 1
            block = jnp.where(step < 4, grid[f, 0, start : start + 8, :], grid[f, 1, start - 4 : start + 4, :])
            out[target, 32 * f : 32 * f + 8, :] = block.astype(BF)
            out[target, 32 * f + 8 : 32 * f + 24, :] = own[target, 16 * f : 16 * f + 16, :]
            block = own[target, 32 + 8 * f : 40 + 8 * f, :].astype(F32)
            block = jnp.where(step < 2, slopes[f, first : first + 8, :], block)
            out[target, 32 * f + 24 : 32 * f + 32, :] = block.astype(BF)
        out[target, 64:72, :] = pieces[...]


def cell_body(
    got, kernel, readout, start, halo, give, keep, stay, grid, decay, gain, taps, driven, states, slopes, drive, turned
):
    sources = got.shape[0]
    count = sources * 16
    wide = (halo.shape[0] - 8) // 6
    lanes = got.shape[2]
    step = sublane((8, lanes))
    is_first = lax.axis_index("row") == 0
    low = jnp.where(is_first & (step < 2), 0.0, 1.0)
    high = jnp.where(is_first & (step >= 4) & (step < 6), 0.0, 1.0)
    near = (step % 4) < 2

    def unpack(source, _):
        for f in range(2):
            grid[2 * source + f] = got[source, 32 * f : 32 * f + 24, :].astype(F32)
        piece = got[source, 64:72, :].astype(F32)
        rate = piece + pltpu.roll(piece, 6, 0) + pltpu.roll(piece, 4, 0)
        decay[source] = rate
        gain[source] = jnp.sqrt(1.0 - rate * rate)
        return _

    lax.fori_loop(0, sources, unpack, 0, unroll=4)

    def gather(source, _):
        rows = pl.ds(pl.multiple_of(16 * source, 16), 16)
        for i in range(3):
            for j in range(3):
                place = 4 * i + j
                pair = []
                for f in range(2):
                    value = jnp.where(
                        near,
                        grid[2 * source + f, place : place + 8, :],
                        grid[2 * source + f, place + 6 : place + 14, :],
                    )
                    if i == 2:
                        value = value * low
                    if i == 0:
                        value = value * high
                    pair.append(value)
                tap = 3 * i + j
                taps[rows, lanes * tap : lanes * tap + lanes] = jnp.concatenate(pair, axis=0).astype(BF)
        return _

    lax.fori_loop(0, sources, gather, 0, unroll=2)

    chunk = min(count, 256)

    def convolve(part, _):
        rows = pl.ds(pl.multiple_of(part * chunk, chunk), chunk)
        driven[rows, :] = jnp.dot(taps[rows, :], kernel[...], preferred_element_type=F32)
        return _

    lax.fori_loop(0, count // chunk, convolve, 0)

    tail = halo[6 * wide : 6 * wide + 8, :].astype(F32)
    tail = tail + pltpu.roll(tail, 6, 0) + pltpu.roll(tail, 4, 0)
    begin = jnp.where(step < 2, tail, start[...])

    def advance(source, state):
        pair = []
        for f in range(2):
            rate = jnp.broadcast_to(decay[source, f : f + 1, :], state.shape)
            size = jnp.broadcast_to(gain[source, f : f + 1, :], state.shape)
            now = driven[pl.ds(pl.multiple_of(16 * source + 8 * f, 8), 8), :]
            state = rate * state + size * now
            pair.append(state)
        states[pl.ds(pl.multiple_of(16 * source, 16), 16), :] = jnp.concatenate(pair, axis=0).astype(BF)
        return state

    lax.fori_loop(0, sources, advance, begin, unroll=4)

    def mix(part, _):
        rows = pl.ds(pl.multiple_of(part * 64, 64), 64)
        mixture = jnp.dot(states[rows, :], readout[...], preferred_element_type=F32)
        upstream = jnp.concatenate(
            [
                got[4 * part + source, 32 * f + 24 : 32 * f + 32, :].astype(F32)
                for source in range(4)
                for f in range(2)
            ],
            axis=0,
        )
        slope = (upstream * gelu_slope(mixture)).astype(BF)
        slopes[rows, :] = slope
        driven[rows, :] = lax.dot_general(
            slope, readout[...], (((1,), (1,)), ((), ())), preferred_element_type=F32
        )
        return _

    lax.fori_loop(0, count // 64, mix, 0, unroll=4)

    def retreat(turn, carried):
        adjoint, later = carried
        source = sources - 1 - turn
        pair = []
        for f in (1, 0):
            now = driven[pl.ds(pl.multiple_of(16 * source + 8 * f, 8), 8), :]
            adjoint = now + later * adjoint
            later = jnp.broadcast_to(decay[source, f : f + 1, :], adjoint.shape)
            value = jnp.broadcast_to(gain[source, f : f + 1, :], adjoint.shape) * adjoint
            pair.append(value)
        drive[pl.ds(pl.multiple_of(16 * source, 16), 16), :] = jnp.concatenate(pair[::-1], axis=0)
        return adjoint, later

    nothing = jnp.zeros((8, lanes), F32)
    lax.fori_loop(0, sources, retreat, (nothing, nothing), unroll=4)

    half = sources // 2
    share = lanes // sources
    is_even = lax.axis_index("tm") % 2 == 0

    def partners_first(value):
        blocks = value.astype(F32).reshape(half, 2, share, count)
        even, odd = blocks[:, 0].reshape(lanes // 2, count), blocks[:, 1].reshape(lanes // 2, count)
        order = (jnp.where(is_even, odd, even), jnp.where(is_even, even, odd))
        return jnp.concatenate(order, axis=0).astype(BF)

    for chip in range(half):
        for f in range(2):
            even = drive[32 * chip + 8 * f : 32 * chip + 8 * f + 8, :]
            odd = drive[32 * chip + 8 * f + 16 : 32 * chip + 8 * f + 24, :]
            columns = slice(10 * lanes + f * lanes, 11 * lanes + f * lanes)
            give[chip, 0:8, columns] = jnp.where(is_even, odd, even).astype(BF)
            stay[chip, :, f * lanes : f * lanes + lanes] = jnp.where(is_even, even, odd).astype(BF)
    turned[...] = partners_first(drive[...].astype(BF).T)
    for tap in range(9):
        columns = slice(lanes * tap, lanes * tap + lanes)
        term = jnp.dot(turned[...], taps[:, columns], preferred_element_type=F32)
        give[:, :, columns] = term[: lanes // 2].astype(BF).reshape(half, share, lanes)
        keep[:, :, columns] = term[lanes // 2 :].reshape(half, share, lanes)
    turned[...] = partners_first(states[...].T)
    columns = slice(9 * lanes, 10 * lanes)
    term = jnp.dot(turned[...], slopes[...], preferred_element_type=F32)
    give[:, :, columns] = term[: lanes // 2].astype(BF).reshape(half, share, lanes)
    keep[:, :, columns] = term[lanes // 2 :].reshape(half, share, lanes)


def merge_body(taken, keep, stay, out):
    lanes = stay.shape[2] // 2
    for chip in range(out.shape[0]):
        total = keep[chip] + taken[chip, :, : 10 * lanes].astype(F32)
        out[chip, :, : 10 * lanes] = total.astype(BF)
    is_even = lax.axis_index("tm") % 2 == 0

    @pl.when(is_even)
    def _():
        out[:, 0:8, 10 * lanes : 12 * lanes] = stay[...]
        out[:, 0:8, 12 * lanes : 14 * lanes] = taken[:, 0:8, 10 * lanes : 12 * lanes]

    @pl.when(jnp.logical_not(is_even))
    def _():
        out[:, 0:8, 10 * lanes : 12 * lanes] = taken[:, 0:8, 10 * lanes : 12 * lanes]
        out[:, 0:8, 12 * lanes : 14 * lanes] = stay[...]


def join_body(bands, got, total, frames, top, cells, grid):
    chips, share, width = got.shape
    sources = 2 * chips
    lanes = width // 14

    def add(source, carried):
        return carried + got[source, :, : 10 * lanes].astype(F32)

    sums = lax.fori_loop(0, chips, add, jnp.zeros((share, 10 * lanes), F32), unroll=2)
    block = lanes // bands
    for band in range(bands):
        total[band] = jnp.concatenate(
            [sums[:, lanes * k + block * band : lanes * k + block * band + block] for k in range(10)], axis=1
        ).astype(BF)

    for f in range(2):
        for part in range(lanes // 128):
            for source in range(sources):
                first = (10 + f + 2 * (source % 2)) * lanes + 128 * part
                cells[8 * source : 8 * source + 8, :] = got[source // 2, 0:8, first : first + 128].astype(F32)
            for place, (row, column) in enumerate(CELLS):
                grid[pl.ds(column, sources, stride=2), :] = cells[pl.ds(place, sources, stride=8), :]
                if column == 1:
                    value = grid[...].astype(BF)
                    frames[f, row, :, 128 * part : 128 * part + 128] = value
                    if row < 2:
                        top[f, row, :, 128 * part : 128 * part + 128] = value


def back_body(first, bands, *refs):
    if first:
        drive, below, kernel, cotangent, feedthrough, _, out, grid, moved, done, sem = refs
    else:
        drive, kernel, cotangent, feedthrough, out, grid, moved, done, sem = refs
    wide, lanes = drive.shape[2:]
    band = lax.axis_index("row")
    for row in range(first, first + 4):
        keep = None
        if row == 0:
            keep = jnp.where(band == 0, 0.0, 1.0)
        if row == 5:
            keep = jnp.where(band == bands - 1, 0.0, 1.0)
        for f in range(2):
            source = (drive[f, row] if row < 4 else below[f, row - 4]).astype(F32)
            if keep is not None:
                source = source * keep
            grid[f, row - first, 0:PAD, :] = jnp.zeros((PAD, lanes), F32)
            grid[f, row - first, PAD + wide :, :] = jnp.zeros((PAD, lanes), F32)
            grid[f, row - first, PAD : PAD + wide, :] = source
            for shift in range(3):
                begin = PAD - 1 + shift
                moved[shift, f, row - first] = grid[f, row - first, begin : begin + wide, :].astype(BF)
    for f in range(2):
        total = jnp.zeros((2 * wide, lanes), F32)
        for i in range(3):
            for j in range(3):
                cells = moved[2 - j, f, 2 - i : 4 - i].reshape(2 * wide, lanes)
                total = total + lax.dot_general(
                    cells, kernel[3 * i + j], (((1,), (1,)), ((), ())), preferred_element_type=F32
                )
        given = cotangent[f, first : first + 2].astype(F32).reshape(2 * wide, lanes)
        done[f] = (total + feedthrough[...] * given).astype(BF).reshape(2, wide, lanes)
    store = pltpu.make_async_copy(done, out.at[:, first : first + 2], sem)
    store.start()
    store.wait()


def sum_body(scaling, got, out):
    total = got[0].astype(F32)
    for band in range(1, got.shape[0]):
        total = total + got[band].astype(F32)
    total = (total * scaling).astype(BF)
    for target in range(out.shape[0]):
        out[target] = total


def last_body(got, kernel_out, readout_out):
    sources, share, width = got.shape
    turned = got[...].astype(F32).reshape(sources * share, width).T
    block = width // 10
    for k in range(9):
        kernel_out[k] = turned[block * k : block * k + block]
    readout_out[...] = turned[9 * block :]


def local(frames_in, cotangent, kernel, readout, feedthrough, decay_rate, start_state):
    here, band_rows, wide, lanes = frames_in.shape
    sources, bands = lax.axis_size("tm"), lax.axis_size("row")
    cells = sources * 16
    share = lanes // sources
    block = lanes // bands
    shape = jax.ShapeDtypeStruct
    down = [(i, (i + 1) % bands) for i in range(bands)]
    up = [((i + 1) % bands, i) for i in range(bands)]

    edge, begin = call(
        halo_body,
        "halo",
        (shape((6 * wide + 8, lanes), BF), shape((8, lanes), F32)),
        [HBM] * 3,
        [
            pltpu.VMEM((2, 2, wide, lanes), BF),
            pltpu.VMEM((2, wide, lanes), BF),
            pltpu.VMEM((4, 8, lanes), F32),
            pltpu.SemaphoreType.DMA((3,)),
        ],
        grant=63 << 20,
    )(frames_in, cotangent, start_state)
    edge = lax.ppermute(edge, "row", down)
    own, pieces = call(
        own_body,
        "own",
        (shape((sources, 48, lanes), BF), shape((8, lanes), BF)),
        [HBM] * 3,
        [
            pltpu.VMEM((2, 4, wide + 2 * PAD, lanes), F32),
            pltpu.VMEM((2, 3, wide + 2 * PAD, lanes), F32),
            pltpu.VMEM((2, 4, wide, lanes), BF),
            pltpu.VMEM((2, 4, wide, lanes), BF),
            pltpu.VMEM((2, lanes), F32),
            pltpu.VMEM((8, lanes), F32),
            pltpu.SemaphoreType.DMA((3,)),
        ],
        moved=8 << 20,
    )(frames_in, cotangent, decay_rate)
    send = call(
        spread_body,
        "spread",
        shape((sources, 72, lanes), BF),
        [VMEM] * 3,
        [
            pltpu.VMEM((2, 2, wide + 2 * PAD, lanes), F32),
            pltpu.VMEM((2, wide + 2 * PAD, lanes), F32),
        ],
    )(own, pieces, edge)
    got = lax.all_to_all(send, "tm", 0, 0)
    half = sources // 2
    give, keep, stay = call(
        cell_body,
        "cells",
        (
            shape((half, share, 12 * lanes), BF),
            shape((half, share, 10 * lanes), F32),
            shape((half, 8, 2 * lanes), BF),
        ),
        [VMEM] * 5,
        [
            pltpu.VMEM((2 * sources, 24, lanes), F32),
            pltpu.VMEM((sources, 8, lanes), F32),
            pltpu.VMEM((sources, 8, lanes), F32),
            pltpu.VMEM((cells, 9 * lanes), BF),
            pltpu.VMEM((cells, lanes), F32),
            pltpu.VMEM((cells, lanes), BF),
            pltpu.VMEM((cells, lanes), BF),
            pltpu.VMEM((cells, lanes), F32),
            pltpu.VMEM((lanes, cells), BF),
        ],
        flops=2 * cells * lanes * lanes * 21,
        moved=4 << 20,
    )(got, kernel.reshape(9 * lanes, lanes), readout, begin, edge)
    taken = lax.ppermute(give, "tm", [(i, i ^ 1) for i in range(sources)])
    send = call(merge_body, "merge", shape((half, share, 14 * lanes), BF), [VMEM] * 3, [])(taken, keep, stay)
    groups = [[2 * chip + core for chip in range(half)] for core in range(2)]
    got = lax.all_to_all(send, "tm", 0, 0, axis_index_groups=groups)
    partial, drive, top = call(
        functools.partial(join_body, bands),
        "join",
        (
            shape((bands, share, 10 * block), BF),
            shape((2, 4, wide, lanes), BF),
            shape((2, 2, wide, lanes), BF),
        ),
        [VMEM],
        [pltpu.VMEM((8 * sources, 128), F32), pltpu.VMEM((wide, 128), F32)],
    )(got)
    below = lax.ppermute(top, "row", up)
    partial = lax.all_to_all(partial, "row", 0, 0)
    scaling = 1.0 / math.sqrt(here * sources * band_rows * bands * wide)
    partial = call(
        functools.partial(sum_body, scaling), "sum", shape((sources, share, 10 * block), BF), [VMEM], []
    )(partial)

    def back(first, ins, **more):
        return call(
            functools.partial(back_body, first, bands),
            "back",
            shape(frames_in.shape, BF),
            ins,
            [
                pltpu.VMEM((2, 4, wide + 2 * PAD, lanes), F32),
                pltpu.VMEM((3, 2, 4, wide, lanes), BF),
                pltpu.VMEM((2, 2, wide, lanes), BF),
                pltpu.SemaphoreType.DMA,
            ],
            flops=cells * lanes * lanes * 9,
            moved=2 << 20,
            to=HBM,
            **more,
        )

    through = feedthrough.reshape(1, lanes)
    grad_frames = back(0, [VMEM] * 4)(drive, kernel, cotangent, through)
    grad_frames = back(2, [VMEM] * 5 + [HBM], alias={5: 0})(
        drive, below, kernel, cotangent, through, grad_frames
    )
    whole = lax.all_to_all(partial, "tm", 0, 0)
    grad_kernel, grad_readout = call(
        last_body, "last", (shape((9, block, lanes), F32), shape((block, lanes), F32)), [VMEM], []
    )(whole)
    return grad_frames, grad_kernel, grad_readout.T


def solution(mesh):
    placed = (
        P("tm", "row", None, None),
        P("tm", "row", None, None),
        P(),
        P(),
        P(),
        P("tm", None),
        P("row", None, None),
    )
    return jax.shard_map(
        local,
        mesh=mesh,
        in_specs=placed,
        out_specs=(P("tm", "row", None, None), P(None, "row", None), P(None, "row")),
        check_vma=False,
    )
```

```python
import functools
import math

import jax
import jax.numpy as jnp
from jax import lax
from jax.experimental import pallas as pl
from jax.experimental.pallas import tpu as pltpu
from jax.sharding import PartitionSpec as P

SQRT_TWO_PI = 0.7978845608
CUBIC = 0.044715
BF = jnp.bfloat16
F32 = jnp.float32
PAD = 8
CELLS = ((0, 0), (0, 1), (1, 0), (1, 1), (2, 0), (2, 1), (3, 0), (3, 1))
VMEM = pl.BlockSpec(memory_space=pltpu.VMEM)
HBM = pl.BlockSpec(memory_space=pltpu.MemorySpace.HBM)


def call(body, name, outs, ins, scratch, flops=1 << 20, moved=1 << 20, grant=40 << 20, to=None, alias=None):
    many = isinstance(outs, (list, tuple))
    return pl.pallas_call(
        body,
        name=name,
        out_shape=outs,
        in_specs=ins,
        out_specs=[VMEM] * len(outs) if many else (to or VMEM),
        input_output_aliases=alias or {},
        scratch_shapes=scratch,
        cost_estimate=pl.CostEstimate(flops=flops, bytes_accessed=moved, transcendentals=0),
        compiler_params=pltpu.CompilerParams(vmem_limit_bytes=grant),
    )


def split3(value):
    high = value.astype(BF).astype(F32)
    rest = value - high
    middle = rest.astype(BF).astype(F32)
    return high, middle, rest - middle


def sublane(shape):
    return lax.broadcasted_iota(jnp.int32, shape, len(shape) - 2)


def gelu_slope(mixture):
    inside = SQRT_TWO_PI * (mixture + CUBIC * mixture * mixture * mixture)
    tangent = jnp.tanh(inside)
    return 0.5 * (1.0 + tangent) + 0.5 * mixture * (1.0 - tangent * tangent) * SQRT_TWO_PI * (
        1.0 + 3.0 * CUBIC * mixture * mixture
    )


def halo_body(frames, cotangent, start, out, begin, rows, slopes, starts, sems):
    wide = frames.shape[2]
    mine = lax.axis_index("tm")
    group = pl.multiple_of(8 * (mine // 4), 8)
    copies = (
        pltpu.make_async_copy(start.at[:, pl.ds(group, 8)], starts, sems.at[0]),
        pltpu.make_async_copy(frames.at[:, 2:4], rows, sems.at[1]),
        pltpu.make_async_copy(cotangent.at[:, 3], slopes, sems.at[2]),
    )
    for copy in copies:
        copy.start()
    for copy in copies:
        copy.wait()
    for f in range(2):
        for row in range(2):
            out[pl.ds((2 * f + row) * wide, wide), :] = rows[f, row]
        out[pl.ds((4 + f) * wide, wide), :] = slopes[f]
    offset = 2 * (mine % 4)
    step = sublane(begin.shape)
    total = jnp.zeros(begin.shape, F32)
    for place, row in ((2, 0), (4, 1), (6, 2)):
        moved = pltpu.roll(starts[row], (8 + place - offset) % 8, 0)
        total = jnp.where((step >= place) & (step < place + 2), moved, total)
    begin[...] = total
    pieces = split3(pltpu.roll(starts[3], (8 - offset) % 8, 0))
    total = jnp.where(step < 2, pieces[0], 0.0)
    total = jnp.where((step >= 2) & (step < 4), pltpu.roll(pieces[1], 2, 0), total)
    total = jnp.where((step >= 4) & (step < 6), pltpu.roll(pieces[2], 4, 0), total)
    out[pl.ds(6 * wide, 8), :] = total.astype(BF)


def places(pair, chips):
    return [(chip, pair - 2 * chip) for chip in range(chips) if 0 <= pair - 2 * chip <= 2]


def own_body(frames, cotangent, decay, out, grid, slopes, rows, given, rates, parts, sems):
    wide, lanes = frames.shape[2:]
    chips = out.shape[0]
    copies = (
        pltpu.make_async_copy(frames, rows, sems.at[0]),
        pltpu.make_async_copy(cotangent, given, sems.at[1]),
        pltpu.make_async_copy(decay, rates, sems.at[2]),
    )
    for copy in copies:
        copy.start()
    for f in range(2):
        for row in range(4):
            grid[f, row, 0:PAD, :] = jnp.zeros((PAD, lanes), F32)
            grid[f, row, PAD + wide :, :] = jnp.zeros((PAD, lanes), F32)
    for copy in copies:
        copy.wait()
    for f in range(2):
        for row in range(4):
            grid[f, row, PAD : PAD + wide, :] = rows[f, row].astype(F32)
        for row in range(3):
            slopes[f, row, PAD : PAD + wide, :] = given[f, row].astype(F32)
    for place, piece in enumerate(split3(rates[...])):
        parts[2 * place : 2 * place + 2, :] = piece
    parts[6:8, :] = jnp.zeros((2, lanes), F32)
    step = sublane((8, lanes))

    def stack(f, terms, first):
        block = None
        for place, row in terms:
            value = grid[f, row, first - place : first - place + 8, :]
            block = value if block is None else jnp.where(step < place, block, value)
        return block.astype(BF)

    for pair in range(wide // 2 + 1):
        first = PAD + 2 * pair - 1
        blocks = (
            stack(0, ((4, 0), (6, 1)), first),
            stack(0, ((0, 2), (2, 3)), first),
            stack(1, ((0, 0), (2, 1), (4, 2), (6, 3)), first),
        )
        for chip, place in places(pair, chips):
            for group in range(3):
                out[chip, 24 * place + 8 * group : 24 * place + 8 * group + 8, :] = blocks[group]
    for target in range(wide // 2):
        first = PAD + 2 * target
        for f in range(2):
            block = slopes[f, 0, first - 2 : first + 6, :]
            for place, row in ((4, 1), (6, 2)):
                block = jnp.where(step < place, block, slopes[f, row, first - place : first - place + 8, :])
            row = 72 + 16 * (target % 2) + 8 * f
            out[target // 2, row : row + 8, :] = block.astype(BF)
    for chip in range(chips):
        out[chip, 104:112, :] = parts[...].astype(BF)


def spread_body(own, halo, out, grid, slopes):
    wide = (halo.shape[0] - 8) // 6
    lanes = halo.shape[1]
    chips = out.shape[0]
    for f in range(2):
        for row in range(2):
            grid[f, row, 0:PAD, :] = jnp.zeros((PAD, lanes), F32)
            grid[f, row, PAD + wide :, :] = jnp.zeros((PAD, lanes), F32)
            grid[f, row, PAD : PAD + wide, :] = halo[pl.ds((2 * f + row) * wide, wide), :].astype(F32)
        slopes[f, PAD : PAD + wide, :] = halo[pl.ds((4 + f) * wide, wide), :].astype(F32)
    step = sublane((8, lanes))
    for pair in range(wide // 2 + 1):
        first = PAD + 2 * pair - 1
        upper = jnp.where(step < 2, grid[0, 0, first : first + 8, :], grid[0, 1, first - 2 : first + 6, :])
        lower = jnp.where(step < 6, grid[1, 0, first - 4 : first + 4, :], grid[1, 1, first - 6 : first + 2, :])
        for chip, place in places(pair, chips):
            row = 24 * place
            block = jnp.where(step < 4, upper, own[chip, row : row + 8, :].astype(F32))
            out[chip, row : row + 8, :] = block.astype(BF)
            block = jnp.where(step < 4, own[chip, row + 8 : row + 16, :].astype(F32), lower)
            out[chip, row + 8 : row + 16, :] = block.astype(BF)
            out[chip, row + 16 : row + 24, :] = own[chip, row + 16 : row + 24, :]
    for target in range(wide // 2):
        first = PAD + 2 * target
        for f in range(2):
            row = 72 + 16 * (target % 2) + 8 * f
            block = own[target // 2, row : row + 8, :].astype(F32)
            block = jnp.where(step < 2, slopes[f, first : first + 8, :], block)
            out[target // 2, row : row + 8, :] = block.astype(BF)
    for chip in range(chips):
        out[chip, 104:112, :] = own[chip, 104:112, :]


def cell_body(
    mine,
    theirs,
    kernel,
    readout,
    start,
    halo,
    give,
    keep,
    stay,
    grid,
    upstream,
    decay,
    gain,
    taps,
    driven,
    states,
    slopes,
    drive,
    turned,
):
    sources = 2 * mine.shape[0]
    count = sources * 16
    wide = (halo.shape[0] - 8) // 6
    lanes = mine.shape[2]
    core = lax.axis_index("tm") % 2
    step = sublane((8, lanes))
    is_first = lax.axis_index("row") == 0
    low = jnp.where(is_first & (step < 2), 0.0, 1.0)
    high = jnp.where(is_first & (step >= 2) & (step < 4), 0.0, 1.0)
    is_left = (step % 2) == 0

    def unpack(chip, _):
        for buffer, other in ((mine, core), (theirs, 1 - core)):
            source = 2 * chip + other
            for part in range(2):
                first = 24 * core + 24 * part
                group = [
                    buffer[chip, pl.ds(pl.multiple_of(first + 8 * g, 8), 8), :].astype(F32) for g in range(3)
                ]
                grid[2 * source, part, 8:16, :] = group[0]
                grid[2 * source, part, 16:24, :] = group[1]
                grid[2 * source + 1, part, 8:16, :] = group[1]
                grid[2 * source + 1, part, 16:24, :] = group[2]
            for f in range(2):
                first = pl.multiple_of(72 + 16 * core + 8 * f, 8)
                upstream[2 * source + f] = buffer[chip, pl.ds(first, 8), :].astype(F32)
            piece = buffer[chip, 104:112, :].astype(F32)
            rate = piece + pltpu.roll(piece, 6, 0) + pltpu.roll(piece, 4, 0)
            decay[source] = rate
            gain[source] = jnp.sqrt(1.0 - rate * rate)
        return _

    lax.fori_loop(0, sources // 2, unpack, 0, unroll=2)

    def gather(source, _):
        rows = pl.ds(pl.multiple_of(16 * source, 16), 16)
        for i in range(3):
            for j in range(3):
                pair = []
                for f in range(2):
                    frame = 2 * source + f
                    first = 8 + 4 * f + 2 * i
                    if j == 1:
                        value = jnp.where(
                            is_left,
                            grid[frame, 0, first + 1 : first + 9, :],
                            grid[frame, 1, first - 1 : first + 7, :],
                        )
                    else:
                        value = grid[frame, j // 2, first : first + 8, :]
                    if i == 2:
                        value = value * low
                    if i == 0:
                        value = value * high
                    pair.append(value)
                tap = 3 * i + j
                taps[rows, lanes * tap : lanes * tap + lanes] = jnp.concatenate(pair, axis=0).astype(BF)
        return _

    lax.fori_loop(0, sources, gather, 0, unroll=2)

    chunk = min(count, 256)

    def convolve(part, _):
        rows = pl.ds(pl.multiple_of(part * chunk, chunk), chunk)
        driven[rows, :] = jnp.dot(taps[rows, :], kernel[...], preferred_element_type=F32)
        return _

    lax.fori_loop(0, count // chunk, convolve, 0)

    tail = halo[6 * wide : 6 * wide + 8, :].astype(F32)
    tail = tail + pltpu.roll(tail, 6, 0) + pltpu.roll(tail, 4, 0)
    begin = jnp.where(step < 2, tail, start[...])

    def advance(source, state):
        pair = []
        for f in range(2):
            rate = jnp.broadcast_to(decay[source, f : f + 1, :], state.shape)
            size = jnp.broadcast_to(gain[source, f : f + 1, :], state.shape)
            now = driven[pl.ds(pl.multiple_of(16 * source + 8 * f, 8), 8), :]
            state = rate * state + size * now
            pair.append(state)
        states[pl.ds(pl.multiple_of(16 * source, 16), 16), :] = jnp.concatenate(pair, axis=0).astype(BF)
        return state

    lax.fori_loop(0, sources, advance, begin, unroll=4)

    def mix(part, _):
        rows = pl.ds(pl.multiple_of(part * 64, 64), 64)
        mixture = jnp.dot(states[rows, :], readout[...], preferred_element_type=F32)
        given = upstream[pl.ds(pl.multiple_of(part * 8, 8), 8)].reshape(64, lanes)
        slope = (given * gelu_slope(mixture)).astype(BF)
        slopes[rows, :] = slope
        driven[rows, :] = lax.dot_general(
            slope, readout[...], (((1,), (1,)), ((), ())), preferred_element_type=F32
        )
        return _

    lax.fori_loop(0, count // 64, mix, 0, unroll=4)

    def retreat(turn, carried):
        adjoint, later = carried
        source = sources - 1 - turn
        pair = []
        for f in (1, 0):
            now = driven[pl.ds(pl.multiple_of(16 * source + 8 * f, 8), 8), :]
            adjoint = now + later * adjoint
            later = jnp.broadcast_to(decay[source, f : f + 1, :], adjoint.shape)
            value = jnp.broadcast_to(gain[source, f : f + 1, :], adjoint.shape) * adjoint
            pair.append(value)
        drive[pl.ds(pl.multiple_of(16 * source, 16), 16), :] = jnp.concatenate(pair[::-1], axis=0)
        return adjoint, later

    nothing = jnp.zeros((8, lanes), F32)
    lax.fori_loop(0, sources, retreat, (nothing, nothing), unroll=4)

    half = sources // 2
    share = lanes // sources
    is_even = lax.axis_index("tm") % 2 == 0

    def partners_first(value):
        blocks = value.astype(F32).reshape(half, 2, share, count)
        even, odd = blocks[:, 0].reshape(lanes // 2, count), blocks[:, 1].reshape(lanes // 2, count)
        order = (jnp.where(is_even, odd, even), jnp.where(is_even, even, odd))
        return jnp.concatenate(order, axis=0).astype(BF)

    for chip in range(half):
        for f in range(2):
            even = drive[32 * chip + 8 * f : 32 * chip + 8 * f + 8, :]
            odd = drive[32 * chip + 8 * f + 16 : 32 * chip + 8 * f + 24, :]
            columns = slice(10 * lanes + f * lanes, 11 * lanes + f * lanes)
            give[chip, 0:8, columns] = jnp.where(is_even, odd, even).astype(BF)
            stay[chip, :, f * lanes : f * lanes + lanes] = jnp.where(is_even, even, odd).astype(BF)
    turned[...] = partners_first(drive[...].astype(BF).T)
    for tap in range(9):
        columns = slice(lanes * tap, lanes * tap + lanes)
        term = jnp.dot(turned[...], taps[:, columns], preferred_element_type=F32)
        give[:, :, columns] = term[: lanes // 2].astype(BF).reshape(half, share, lanes)
        keep[:, :, columns] = term[lanes // 2 :].reshape(half, share, lanes)
    turned[...] = partners_first(states[...].T)
    columns = slice(9 * lanes, 10 * lanes)
    term = jnp.dot(turned[...], slopes[...], preferred_element_type=F32)
    give[:, :, columns] = term[: lanes // 2].astype(BF).reshape(half, share, lanes)
    keep[:, :, columns] = term[lanes // 2 :].reshape(half, share, lanes)


def merge_body(taken, keep, stay, out):
    lanes = stay.shape[2] // 2
    for chip in range(out.shape[0]):
        total = keep[chip] + taken[chip, :, : 10 * lanes].astype(F32)
        out[chip, :, : 10 * lanes] = total.astype(BF)
    is_even = lax.axis_index("tm") % 2 == 0

    @pl.when(is_even)
    def _():
        out[:, 0:8, 10 * lanes : 12 * lanes] = stay[...]
        out[:, 0:8, 12 * lanes : 14 * lanes] = taken[:, 0:8, 10 * lanes : 12 * lanes]

    @pl.when(jnp.logical_not(is_even))
    def _():
        out[:, 0:8, 10 * lanes : 12 * lanes] = taken[:, 0:8, 10 * lanes : 12 * lanes]
        out[:, 0:8, 12 * lanes : 14 * lanes] = stay[...]


def join_body(bands, got, total, frames, top, cells, grid):
    chips, share, width = got.shape
    sources = 2 * chips
    lanes = width // 14

    def add(source, carried):
        return carried + got[source, :, : 10 * lanes].astype(F32)

    sums = lax.fori_loop(0, chips, add, jnp.zeros((share, 10 * lanes), F32), unroll=2)
    block = lanes // bands
    for band in range(bands):
        total[band] = jnp.concatenate(
            [sums[:, lanes * k + block * band : lanes * k + block * band + block] for k in range(10)], axis=1
        ).astype(BF)

    for f in range(2):
        for part in range(lanes // 128):
            for source in range(sources):
                first = (10 + f + 2 * (source % 2)) * lanes + 128 * part
                cells[8 * source : 8 * source + 8, :] = got[source // 2, 0:8, first : first + 128].astype(F32)
            for place, (row, column) in enumerate(CELLS):
                grid[pl.ds(column, sources, stride=2), :] = cells[pl.ds(place, sources, stride=8), :]
                if column == 1:
                    value = grid[...].astype(BF)
                    frames[f, row, :, 128 * part : 128 * part + 128] = value
                    if row < 2:
                        top[f, row, :, 128 * part : 128 * part + 128] = value


def back_body(first, bands, *refs):
    if first:
        drive, below, kernel, cotangent, feedthrough, _, out, grid, moved, done, sem = refs
    else:
        drive, kernel, cotangent, feedthrough, out, grid, moved, done, sem = refs
    wide, lanes = drive.shape[2:]
    band = lax.axis_index("row")
    for row in range(first, first + 4):
        keep = None
        if row == 0:
            keep = jnp.where(band == 0, 0.0, 1.0)
        if row == 5:
            keep = jnp.where(band == bands - 1, 0.0, 1.0)
        for f in range(2):
            source = (drive[f, row] if row < 4 else below[f, row - 4]).astype(F32)
            if keep is not None:
                source = source * keep
            grid[f, row - first, 0:PAD, :] = jnp.zeros((PAD, lanes), F32)
            grid[f, row - first, PAD + wide :, :] = jnp.zeros((PAD, lanes), F32)
            grid[f, row - first, PAD : PAD + wide, :] = source
            for shift in range(3):
                begin = PAD - 1 + shift
                moved[shift, f, row - first] = grid[f, row - first, begin : begin + wide, :].astype(BF)
    for f in range(2):
        total = jnp.zeros((2 * wide, lanes), F32)
        for i in range(3):
            for j in range(3):
                cells = moved[2 - j, f, 2 - i : 4 - i].reshape(2 * wide, lanes)
                total = total + lax.dot_general(
                    cells, kernel[3 * i + j], (((1,), (1,)), ((), ())), preferred_element_type=F32
                )
        given = cotangent[f, first : first + 2].astype(F32).reshape(2 * wide, lanes)
        done[f] = (total + feedthrough[...] * given).astype(BF).reshape(2, wide, lanes)
    store = pltpu.make_async_copy(done, out.at[:, first : first + 2], sem)
    store.start()
    store.wait()


def sum_body(scaling, got, out):
    total = got[0].astype(F32)
    for band in range(1, got.shape[0]):
        total = total + got[band].astype(F32)
    total = (total * scaling).astype(BF)
    for target in range(out.shape[0]):
        out[target] = total


def last_body(got, kernel_out, readout_out):
    sources, share, width = got.shape
    turned = got[...].astype(F32).reshape(sources * share, width).T
    block = width // 10
    for k in range(9):
        kernel_out[k] = turned[block * k : block * k + block]
    readout_out[...] = turned[9 * block :]


def local(frames_in, cotangent, kernel, readout, feedthrough, decay_rate, start_state):
    here, band_rows, wide, lanes = frames_in.shape
    sources, bands = lax.axis_size("tm"), lax.axis_size("row")
    cells = sources * 16
    share = lanes // sources
    block = lanes // bands
    shape = jax.ShapeDtypeStruct
    down = [(i, (i + 1) % bands) for i in range(bands)]
    up = [((i + 1) % bands, i) for i in range(bands)]

    edge, begin = call(
        halo_body,
        "halo",
        (shape((6 * wide + 8, lanes), BF), shape((8, lanes), F32)),
        [HBM] * 3,
        [
            pltpu.VMEM((2, 2, wide, lanes), BF),
            pltpu.VMEM((2, wide, lanes), BF),
            pltpu.VMEM((4, 8, lanes), F32),
            pltpu.SemaphoreType.DMA((3,)),
        ],
        grant=63 << 20,
    )(frames_in, cotangent, start_state)
    edge = lax.ppermute(edge, "row", down)
    half = sources // 2
    groups = [[2 * chip + core for chip in range(half)] for core in range(2)]
    swap = [(i, i ^ 1) for i in range(sources)]
    own = call(
        own_body,
        "own",
        shape((half, 112, lanes), BF),
        [HBM] * 3,
        [
            pltpu.VMEM((2, 4, wide + 2 * PAD, lanes), F32),
            pltpu.VMEM((2, 3, wide + 2 * PAD, lanes), F32),
            pltpu.VMEM((2, 4, wide, lanes), BF),
            pltpu.VMEM((2, 4, wide, lanes), BF),
            pltpu.VMEM((2, lanes), F32),
            pltpu.VMEM((8, lanes), F32),
            pltpu.SemaphoreType.DMA((3,)),
        ],
        moved=8 << 20,
    )(frames_in, cotangent, decay_rate)
    send = call(
        spread_body,
        "spread",
        shape((half, 112, lanes), BF),
        [VMEM] * 2,
        [
            pltpu.VMEM((2, 2, wide + 2 * PAD, lanes), F32),
            pltpu.VMEM((2, wide + 2 * PAD, lanes), F32),
        ],
    )(own, edge)
    mine = lax.all_to_all(send, "tm", 0, 0, axis_index_groups=groups)
    theirs = lax.ppermute(mine, "tm", swap)
    give, keep, stay = call(
        cell_body,
        "cells",
        (
            shape((half, share, 12 * lanes), BF),
            shape((half, share, 10 * lanes), F32),
            shape((half, 8, 2 * lanes), BF),
        ),
        [VMEM] * 6,
        [
            pltpu.VMEM((2 * sources, 2, 32, lanes), F32),
            pltpu.VMEM((2 * sources, 8, lanes), F32),
            pltpu.VMEM((sources, 8, lanes), F32),
            pltpu.VMEM((sources, 8, lanes), F32),
            pltpu.VMEM((cells, 9 * lanes), BF),
            pltpu.VMEM((cells, lanes), F32),
            pltpu.VMEM((cells, lanes), BF),
            pltpu.VMEM((cells, lanes), BF),
            pltpu.VMEM((cells, lanes), F32),
            pltpu.VMEM((lanes, cells), BF),
        ],
        flops=2 * cells * lanes * lanes * 21,
        moved=4 << 20,
    )(mine, theirs, kernel.reshape(9 * lanes, lanes), readout, begin, edge)
    taken = lax.ppermute(give, "tm", swap)
    send = call(merge_body, "merge", shape((half, share, 14 * lanes), BF), [VMEM] * 3, [])(taken, keep, stay)
    got = lax.all_to_all(send, "tm", 0, 0, axis_index_groups=groups)
    partial, drive, top = call(
        functools.partial(join_body, bands),
        "join",
        (
            shape((bands, share, 10 * block), BF),
            shape((2, 4, wide, lanes), BF),
            shape((2, 2, wide, lanes), BF),
        ),
        [VMEM],
        [pltpu.VMEM((8 * sources, 128), F32), pltpu.VMEM((wide, 128), F32)],
    )(got)
    below = lax.ppermute(top, "row", up)
    partial = lax.all_to_all(partial, "row", 0, 0)
    scaling = 1.0 / math.sqrt(here * sources * band_rows * bands * wide)
    partial = call(
        functools.partial(sum_body, scaling), "sum", shape((sources, share, 10 * block), BF), [VMEM], []
    )(partial)

    def back(first, ins, **more):
        return call(
            functools.partial(back_body, first, bands),
            "back",
            shape(frames_in.shape, BF),
            ins,
            [
                pltpu.VMEM((2, 4, wide + 2 * PAD, lanes), F32),
                pltpu.VMEM((3, 2, 4, wide, lanes), BF),
                pltpu.VMEM((2, 2, wide, lanes), BF),
                pltpu.SemaphoreType.DMA,
            ],
            flops=cells * lanes * lanes * 9,
            moved=2 << 20,
            to=HBM,
            **more,
        )

    through = feedthrough.reshape(1, lanes)
    grad_frames = back(0, [VMEM] * 4)(drive, kernel, cotangent, through)
    grad_frames = back(2, [VMEM] * 5 + [HBM], alias={5: 0})(
        drive, below, kernel, cotangent, through, grad_frames
    )
    whole = lax.all_to_all(partial, "tm", 0, 0)
    grad_kernel, grad_readout = call(
        last_body, "last", (shape((9, block, lanes), F32), shape((block, lanes), F32)), [VMEM], []
    )(whole)
    return grad_frames, grad_kernel, grad_readout.T


def solution(mesh):
    placed = (
        P("tm", "row", None, None),
        P("tm", "row", None, None),
        P(),
        P(),
        P(),
        P("tm", None),
        P("row", None, None),
    )
    return jax.shard_map(
        local,
        mesh=mesh,
        in_specs=placed,
        out_specs=(P("tm", "row", None, None), P(None, "row", None), P(None, "row")),
        check_vma=False,
    )
```

```python
import functools
import math

import jax
import jax.numpy as jnp
from jax import lax
from jax.experimental import pallas as pl
from jax.experimental.pallas import tpu as pltpu
from jax.sharding import PartitionSpec as P

SQRT_TWO_PI = 0.7978845608
CUBIC = 0.044715
BF = jnp.bfloat16
F32 = jnp.float32
PAD = 8
CELLS = ((0, 0), (0, 1), (1, 0), (1, 1), (2, 0), (2, 1), (3, 0), (3, 1))
VMEM = pl.BlockSpec(memory_space=pltpu.VMEM)
HBM = pl.BlockSpec(memory_space=pltpu.MemorySpace.HBM)


def call(body, name, outs, ins, scratch, flops=1 << 20, moved=1 << 20, grant=40 << 20, to=None, alias=None):
    many = isinstance(outs, (list, tuple))
    return pl.pallas_call(
        body,
        name=name,
        out_shape=outs,
        in_specs=ins,
        out_specs=[VMEM] * len(outs) if many else (to or VMEM),
        input_output_aliases=alias or {},
        scratch_shapes=scratch,
        cost_estimate=pl.CostEstimate(flops=flops, bytes_accessed=moved, transcendentals=0),
        compiler_params=pltpu.CompilerParams(vmem_limit_bytes=grant),
    )


def split3(value):
    high = value.astype(BF).astype(F32)
    rest = value - high
    middle = rest.astype(BF).astype(F32)
    return high, middle, rest - middle


def sublane(shape):
    return lax.broadcasted_iota(jnp.int32, shape, len(shape) - 2)


def gelu_slope(mixture):
    inside = SQRT_TWO_PI * (mixture + CUBIC * mixture * mixture * mixture)
    tangent = jnp.tanh(inside)
    return 0.5 * (1.0 + tangent) + 0.5 * mixture * (1.0 - tangent * tangent) * SQRT_TWO_PI * (
        1.0 + 3.0 * CUBIC * mixture * mixture
    )


def halo_body(frames, cotangent, start, out, begin, rows, slopes, starts, sems):
    wide = frames.shape[2]
    mine = lax.axis_index("tm")
    group = pl.multiple_of(8 * (mine // 4), 8)
    copies = (
        pltpu.make_async_copy(start.at[:, pl.ds(group, 8)], starts, sems.at[0]),
        pltpu.make_async_copy(frames.at[:, 2:4], rows, sems.at[1]),
        pltpu.make_async_copy(cotangent.at[:, 3], slopes, sems.at[2]),
    )
    for copy in copies:
        copy.start()
    for copy in copies:
        copy.wait()
    for f in range(2):
        for row in range(2):
            out[pl.ds((2 * f + row) * wide, wide), :] = rows[f, row]
        out[pl.ds((4 + f) * wide, wide), :] = slopes[f]
    offset = 2 * (mine % 4)
    step = sublane(begin.shape)
    total = jnp.zeros(begin.shape, F32)
    for place, row in ((2, 0), (4, 1), (6, 2)):
        moved = pltpu.roll(starts[row], (8 + place - offset) % 8, 0)
        total = jnp.where((step >= place) & (step < place + 2), moved, total)
    begin[...] = total
    pieces = split3(pltpu.roll(starts[3], (8 - offset) % 8, 0))
    total = jnp.where(step < 2, pieces[0], 0.0)
    total = jnp.where((step >= 2) & (step < 4), pltpu.roll(pieces[1], 2, 0), total)
    total = jnp.where((step >= 4) & (step < 6), pltpu.roll(pieces[2], 4, 0), total)
    out[pl.ds(6 * wide, 8), :] = total.astype(BF)


def places(pair, chips):
    return [(chip, pair - 2 * chip) for chip in range(chips) if 0 <= pair - 2 * chip <= 2]


def own_body(frames, cotangent, decay, out, grid, slopes, rows, given, rates, parts, sems):
    wide, lanes = frames.shape[2:]
    chips = out.shape[0]
    copies = (
        pltpu.make_async_copy(frames, rows, sems.at[0]),
        pltpu.make_async_copy(cotangent, given, sems.at[1]),
        pltpu.make_async_copy(decay, rates, sems.at[2]),
    )
    for copy in copies:
        copy.start()
    for f in range(2):
        for row in range(4):
            grid[f, row, 0:PAD, :] = jnp.zeros((PAD, lanes), F32)
            grid[f, row, PAD + wide :, :] = jnp.zeros((PAD, lanes), F32)
    for copy in copies:
        copy.wait()
    for f in range(2):
        for row in range(4):
            grid[f, row, PAD : PAD + wide, :] = rows[f, row].astype(F32)
        for row in range(3):
            slopes[f, row, PAD : PAD + wide, :] = given[f, row].astype(F32)
    for place, piece in enumerate(split3(rates[...])):
        parts[2 * place : 2 * place + 2, :] = piece
    parts[6:8, :] = jnp.zeros((2, lanes), F32)
    step = sublane((8, lanes))

    def stack(f, terms, first):
        block = None
        for place, row in terms:
            value = grid[f, row, first - place : first - place + 8, :]
            block = value if block is None else jnp.where(step < place, block, value)
        return block.astype(BF)

    for pair in range(wide // 2 + 1):
        first = PAD + 2 * pair - 1
        blocks = (
            stack(0, ((4, 0), (6, 1)), first),
            stack(0, ((0, 2), (2, 3)), first),
            stack(1, ((0, 0), (2, 1), (4, 2), (6, 3)), first),
        )
        for chip, place in places(pair, chips):
            for group in range(3):
                out[chip, 24 * place + 8 * group : 24 * place + 8 * group + 8, :] = blocks[group]
    for target in range(wide // 2):
        first = PAD + 2 * target
        for f in range(2):
            block = slopes[f, 0, first - 2 : first + 6, :]
            for place, row in ((4, 1), (6, 2)):
                block = jnp.where(step < place, block, slopes[f, row, first - place : first - place + 8, :])
            row = 72 + 16 * (target % 2) + 8 * f
            out[target // 2, row : row + 8, :] = block.astype(BF)
    for chip in range(chips):
        out[chip, 104:112, :] = parts[...].astype(BF)


def spread_body(own, halo, out, grid, slopes):
    wide = (halo.shape[0] - 8) // 6
    lanes = halo.shape[1]
    chips = out.shape[0]
    for f in range(2):
        for row in range(2):
            grid[f, row, 0:PAD, :] = jnp.zeros((PAD, lanes), F32)
            grid[f, row, PAD + wide :, :] = jnp.zeros((PAD, lanes), F32)
            grid[f, row, PAD : PAD + wide, :] = halo[pl.ds((2 * f + row) * wide, wide), :].astype(F32)
        slopes[f, PAD : PAD + wide, :] = halo[pl.ds((4 + f) * wide, wide), :].astype(F32)
    step = sublane((8, lanes))
    for pair in range(wide // 2 + 1):
        first = PAD + 2 * pair - 1
        upper = jnp.where(step < 2, grid[0, 0, first : first + 8, :], grid[0, 1, first - 2 : first + 6, :])
        lower = jnp.where(step < 6, grid[1, 0, first - 4 : first + 4, :], grid[1, 1, first - 6 : first + 2, :])
        for chip, place in places(pair, chips):
            row = 24 * place
            block = jnp.where(step < 4, upper, own[chip, row : row + 8, :].astype(F32))
            out[chip, row : row + 8, :] = block.astype(BF)
            block = jnp.where(step < 4, own[chip, row + 8 : row + 16, :].astype(F32), lower)
            out[chip, row + 8 : row + 16, :] = block.astype(BF)
            out[chip, row + 16 : row + 24, :] = own[chip, row + 16 : row + 24, :]
    for target in range(wide // 2):
        first = PAD + 2 * target
        for f in range(2):
            row = 72 + 16 * (target % 2) + 8 * f
            block = own[target // 2, row : row + 8, :].astype(F32)
            block = jnp.where(step < 2, slopes[f, first : first + 8, :], block)
            out[target // 2, row : row + 8, :] = block.astype(BF)
    for chip in range(chips):
        out[chip, 104:112, :] = own[chip, 104:112, :]


def cell_body(
    mine,
    theirs,
    kernel,
    readout,
    start,
    halo,
    give,
    keep,
    stay,
    grid,
    upstream,
    decay,
    gain,
    taps,
    driven,
    states,
    slopes,
    drive,
    turned,
):
    sources = 2 * mine.shape[0]
    count = sources * 16
    wide = (halo.shape[0] - 8) // 6
    lanes = mine.shape[2]
    core = lax.axis_index("tm") % 2
    step = sublane((8, lanes))
    is_first = lax.axis_index("row") == 0
    low = jnp.where(is_first & (step < 2), 0.0, 1.0)
    high = jnp.where(is_first & (step >= 2) & (step < 4), 0.0, 1.0)
    is_left = (step % 2) == 0

    def unpack(chip, _):
        for buffer, other in ((mine, core), (theirs, 1 - core)):
            source = 2 * chip + other
            for part in range(2):
                first = 24 * core + 24 * part
                group = [
                    buffer[chip, pl.ds(pl.multiple_of(first + 8 * g, 8), 8), :].astype(F32) for g in range(3)
                ]
                grid[2 * source, part, 8:16, :] = group[0]
                grid[2 * source, part, 16:24, :] = group[1]
                grid[2 * source + 1, part, 8:16, :] = group[1]
                grid[2 * source + 1, part, 16:24, :] = group[2]
            for f in range(2):
                first = pl.multiple_of(72 + 16 * core + 8 * f, 8)
                upstream[2 * source + f] = buffer[chip, pl.ds(first, 8), :].astype(F32)
            piece = buffer[chip, 104:112, :].astype(F32)
            rate = piece + pltpu.roll(piece, 6, 0) + pltpu.roll(piece, 4, 0)
            decay[source] = rate
            gain[source] = jnp.sqrt(1.0 - rate * rate)
        return _

    lax.fori_loop(0, sources // 2, unpack, 0, unroll=2)

    def gather(source, _):
        rows = pl.ds(pl.multiple_of(16 * source, 16), 16)
        for i in range(3):
            for j in range(3):
                pair = []
                for f in range(2):
                    frame = 2 * source + f
                    first = 8 + 4 * f + 2 * i
                    if j == 1:
                        value = jnp.where(
                            is_left,
                            grid[frame, 0, first + 1 : first + 9, :],
                            grid[frame, 1, first - 1 : first + 7, :],
                        )
                    else:
                        value = grid[frame, j // 2, first : first + 8, :]
                    if i == 2:
                        value = value * low
                    if i == 0:
                        value = value * high
                    pair.append(value)
                tap = 3 * i + j
                taps[rows, lanes * tap : lanes * tap + lanes] = jnp.concatenate(pair, axis=0).astype(BF)
        return _

    chunk = min(count, 128)
    for part in range(count // chunk):
        for source in range(chunk // 16):
            gather(part * (chunk // 16) + source, 0)
        rows = slice(part * chunk, part * chunk + chunk)
        driven[rows, :] = jnp.dot(taps[rows, :], kernel[...], preferred_element_type=F32)

    tail = halo[6 * wide : 6 * wide + 8, :].astype(F32)
    tail = tail + pltpu.roll(tail, 6, 0) + pltpu.roll(tail, 4, 0)
    begin = jnp.where(step < 2, tail, start[...])

    def advance(source, state):
        pair = []
        for f in range(2):
            rate = jnp.broadcast_to(decay[source, f : f + 1, :], state.shape)
            size = jnp.broadcast_to(gain[source, f : f + 1, :], state.shape)
            now = driven[pl.ds(pl.multiple_of(16 * source + 8 * f, 8), 8), :]
            state = rate * state + size * now
            pair.append(state)
        states[pl.ds(pl.multiple_of(16 * source, 16), 16), :] = jnp.concatenate(pair, axis=0).astype(BF)
        return state

    lax.fori_loop(0, sources, advance, begin, unroll=4)

    def mix(part, _):
        rows = pl.ds(pl.multiple_of(part * 64, 64), 64)
        mixture = jnp.dot(states[rows, :], readout[...], preferred_element_type=F32)
        given = upstream[pl.ds(pl.multiple_of(part * 8, 8), 8)].reshape(64, lanes)
        slope = (given * gelu_slope(mixture)).astype(BF)
        slopes[rows, :] = slope
        driven[rows, :] = lax.dot_general(
            slope, readout[...], (((1,), (1,)), ((), ())), preferred_element_type=F32
        )
        return _

    lax.fori_loop(0, count // 64, mix, 0, unroll=8)

    def retreat(turn, carried):
        adjoint, later = carried
        source = sources - 1 - turn
        pair = []
        for f in (1, 0):
            now = driven[pl.ds(pl.multiple_of(16 * source + 8 * f, 8), 8), :]
            adjoint = now + later * adjoint
            later = jnp.broadcast_to(decay[source, f : f + 1, :], adjoint.shape)
            value = jnp.broadcast_to(gain[source, f : f + 1, :], adjoint.shape) * adjoint
            pair.append(value)
        drive[pl.ds(pl.multiple_of(16 * source, 16), 16), :] = jnp.concatenate(pair[::-1], axis=0)
        return adjoint, later

    nothing = jnp.zeros((8, lanes), F32)
    lax.fori_loop(0, sources, retreat, (nothing, nothing), unroll=4)

    half = sources // 2
    share = lanes // sources
    is_even = lax.axis_index("tm") % 2 == 0

    def partners_first(value):
        blocks = value.astype(F32).reshape(half, 2, share, count)
        even, odd = blocks[:, 0].reshape(lanes // 2, count), blocks[:, 1].reshape(lanes // 2, count)
        order = (jnp.where(is_even, odd, even), jnp.where(is_even, even, odd))
        return jnp.concatenate(order, axis=0).astype(BF)

    for chip in range(half):
        for f in range(2):
            even = drive[32 * chip + 8 * f : 32 * chip + 8 * f + 8, :]
            odd = drive[32 * chip + 8 * f + 16 : 32 * chip + 8 * f + 24, :]
            columns = slice(10 * lanes + f * lanes, 11 * lanes + f * lanes)
            give[chip, 0:8, columns] = jnp.where(is_even, odd, even).astype(BF)
            stay[chip, :, f * lanes : f * lanes + lanes] = jnp.where(is_even, even, odd).astype(BF)
    turned[...] = partners_first(drive[...].astype(BF).T)
    for tap in range(9):
        columns = slice(lanes * tap, lanes * tap + lanes)
        term = jnp.dot(turned[...], taps[:, columns], preferred_element_type=F32)
        give[:, :, columns] = term[: lanes // 2].astype(BF).reshape(half, share, lanes)
        keep[:, :, columns] = term[lanes // 2 :].reshape(half, share, lanes)
    turned[...] = partners_first(states[...].T)
    columns = slice(9 * lanes, 10 * lanes)
    term = jnp.dot(turned[...], slopes[...], preferred_element_type=F32)
    give[:, :, columns] = term[: lanes // 2].astype(BF).reshape(half, share, lanes)
    keep[:, :, columns] = term[lanes // 2 :].reshape(half, share, lanes)


def merge_body(taken, keep, stay, out):
    lanes = stay.shape[2] // 2
    for chip in range(out.shape[0]):
        total = keep[chip] + taken[chip, :, : 10 * lanes].astype(F32)
        out[chip, :, : 10 * lanes] = total.astype(BF)
    is_even = lax.axis_index("tm") % 2 == 0

    @pl.when(is_even)
    def _():
        out[:, 0:8, 10 * lanes : 12 * lanes] = stay[...]
        out[:, 0:8, 12 * lanes : 14 * lanes] = taken[:, 0:8, 10 * lanes : 12 * lanes]

    @pl.when(jnp.logical_not(is_even))
    def _():
        out[:, 0:8, 10 * lanes : 12 * lanes] = taken[:, 0:8, 10 * lanes : 12 * lanes]
        out[:, 0:8, 12 * lanes : 14 * lanes] = stay[...]


def join_body(bands, got, total, frames, top, cells, grid):
    chips, share, width = got.shape
    sources = 2 * chips
    lanes = width // 14

    def add(source, carried):
        return carried + got[source, :, : 10 * lanes].astype(F32)

    sums = lax.fori_loop(0, chips, add, jnp.zeros((share, 10 * lanes), F32), unroll=2)
    block = lanes // bands
    for band in range(bands):
        total[band] = jnp.concatenate(
            [sums[:, lanes * k + block * band : lanes * k + block * band + block] for k in range(10)], axis=1
        ).astype(BF)

    for f in range(2):
        for part in range(lanes // 128):
            for source in range(sources):
                first = (10 + f + 2 * (source % 2)) * lanes + 128 * part
                cells[8 * source : 8 * source + 8, :] = got[source // 2, 0:8, first : first + 128].astype(F32)
            for place, (row, column) in enumerate(CELLS):
                grid[pl.ds(column, sources, stride=2), :] = cells[pl.ds(place, sources, stride=8), :]
                if column == 1:
                    value = grid[...].astype(BF)
                    frames[f, row, :, 128 * part : 128 * part + 128] = value
                    if row < 2:
                        top[f, row, :, 128 * part : 128 * part + 128] = value


def back_body(first, bands, *refs):
    if first:
        drive, below, kernel, cotangent, feedthrough, _, out, grid, moved, done, sem = refs
    else:
        drive, kernel, cotangent, feedthrough, out, grid, moved, done, sem = refs
    wide, lanes = drive.shape[2:]
    band = lax.axis_index("row")
    for row in range(first, first + 4):
        keep = None
        if row == 0:
            keep = jnp.where(band == 0, 0.0, 1.0)
        if row == 5:
            keep = jnp.where(band == bands - 1, 0.0, 1.0)
        for f in range(2):
            source = (drive[f, row] if row < 4 else below[f, row - 4]).astype(F32)
            if keep is not None:
                source = source * keep
            grid[f, row - first, 0:PAD, :] = jnp.zeros((PAD, lanes), F32)
            grid[f, row - first, PAD + wide :, :] = jnp.zeros((PAD, lanes), F32)
            grid[f, row - first, PAD : PAD + wide, :] = source
            for shift in range(3):
                begin = PAD - 1 + shift
                moved[shift, f, row - first] = grid[f, row - first, begin : begin + wide, :].astype(BF)
    for f in range(2):
        total = jnp.zeros((2 * wide, lanes), F32)
        for i in range(3):
            for j in range(3):
                cells = moved[2 - j, f, 2 - i : 4 - i].reshape(2 * wide, lanes)
                total = total + lax.dot_general(
                    cells, kernel[3 * i + j], (((1,), (1,)), ((), ())), preferred_element_type=F32
                )
        given = cotangent[f, first : first + 2].astype(F32).reshape(2 * wide, lanes)
        done[f] = (total + feedthrough[...] * given).astype(BF).reshape(2, wide, lanes)
    store = pltpu.make_async_copy(done, out.at[:, first : first + 2], sem)
    store.start()
    store.wait()


def sum_body(scaling, got, out):
    total = got[0].astype(F32)
    for band in range(1, got.shape[0]):
        total = total + got[band].astype(F32)
    total = (total * scaling).astype(BF)
    for target in range(out.shape[0]):
        out[target] = total


def last_body(mine, theirs, kernel_out, readout_out):
    chips, share, width = mine.shape
    is_even = lax.axis_index("tm") % 2 == 0
    here, there = mine[...].astype(F32), theirs[...].astype(F32)
    pairs = [jnp.where(is_even, here, there), jnp.where(is_even, there, here)]
    turned = jnp.stack(pairs, axis=1).reshape(2 * chips * share, width).T
    block = width // 10
    for k in range(9):
        kernel_out[k] = turned[block * k : block * k + block]
    readout_out[...] = turned[9 * block :]


def local(frames_in, cotangent, kernel, readout, feedthrough, decay_rate, start_state):
    here, band_rows, wide, lanes = frames_in.shape
    sources, bands = lax.axis_size("tm"), lax.axis_size("row")
    cells = sources * 16
    share = lanes // sources
    block = lanes // bands
    shape = jax.ShapeDtypeStruct
    down = [(i, (i + 1) % bands) for i in range(bands)]
    up = [((i + 1) % bands, i) for i in range(bands)]

    edge, begin = call(
        halo_body,
        "halo",
        (shape((6 * wide + 8, lanes), BF), shape((8, lanes), F32)),
        [HBM] * 3,
        [
            pltpu.VMEM((2, 2, wide, lanes), BF),
            pltpu.VMEM((2, wide, lanes), BF),
            pltpu.VMEM((4, 8, lanes), F32),
            pltpu.SemaphoreType.DMA((3,)),
        ],
        grant=63 << 20,
    )(frames_in, cotangent, start_state)
    edge = lax.ppermute(edge, "row", down)
    half = sources // 2
    groups = [[2 * chip + core for chip in range(half)] for core in range(2)]
    swap = [(i, i ^ 1) for i in range(sources)]
    own = call(
        own_body,
        "own",
        shape((half, 112, lanes), BF),
        [HBM] * 3,
        [
            pltpu.VMEM((2, 4, wide + 2 * PAD, lanes), F32),
            pltpu.VMEM((2, 3, wide + 2 * PAD, lanes), F32),
            pltpu.VMEM((2, 4, wide, lanes), BF),
            pltpu.VMEM((2, 4, wide, lanes), BF),
            pltpu.VMEM((2, lanes), F32),
            pltpu.VMEM((8, lanes), F32),
            pltpu.SemaphoreType.DMA((3,)),
        ],
        moved=8 << 20,
    )(frames_in, cotangent, decay_rate)
    send = call(
        spread_body,
        "spread",
        shape((half, 112, lanes), BF),
        [VMEM] * 2,
        [
            pltpu.VMEM((2, 2, wide + 2 * PAD, lanes), F32),
            pltpu.VMEM((2, wide + 2 * PAD, lanes), F32),
        ],
    )(own, edge)
    mine = lax.all_to_all(send, "tm", 0, 0, axis_index_groups=groups)
    theirs = lax.ppermute(mine, "tm", swap)
    give, keep, stay = call(
        cell_body,
        "cells",
        (
            shape((half, share, 12 * lanes), BF),
            shape((half, share, 10 * lanes), F32),
            shape((half, 8, 2 * lanes), BF),
        ),
        [VMEM] * 6,
        [
            pltpu.VMEM((2 * sources, 2, 32, lanes), F32),
            pltpu.VMEM((2 * sources, 8, lanes), F32),
            pltpu.VMEM((sources, 8, lanes), F32),
            pltpu.VMEM((sources, 8, lanes), F32),
            pltpu.VMEM((cells, 9 * lanes), BF),
            pltpu.VMEM((cells, lanes), F32),
            pltpu.VMEM((cells, lanes), BF),
            pltpu.VMEM((cells, lanes), BF),
            pltpu.VMEM((cells, lanes), F32),
            pltpu.VMEM((lanes, cells), BF),
        ],
        flops=2 * cells * lanes * lanes * 21,
        moved=4 << 20,
    )(mine, theirs, kernel.reshape(9 * lanes, lanes), readout, begin, edge)
    taken = lax.ppermute(give, "tm", swap)
    send = call(merge_body, "merge", shape((half, share, 14 * lanes), BF), [VMEM] * 3, [])(taken, keep, stay)
    got = lax.all_to_all(send, "tm", 0, 0, axis_index_groups=groups)
    partial, drive, top = call(
        functools.partial(join_body, bands),
        "join",
        (
            shape((bands, share, 10 * block), BF),
            shape((2, 4, wide, lanes), BF),
            shape((2, 2, wide, lanes), BF),
        ),
        [VMEM],
        [pltpu.VMEM((8 * sources, 128), F32), pltpu.VMEM((wide, 128), F32)],
    )(got)
    below = lax.ppermute(top, "row", up)
    partial = lax.all_to_all(partial, "row", 0, 0)
    scaling = 1.0 / math.sqrt(here * sources * band_rows * bands * wide)
    partial = call(
        functools.partial(sum_body, scaling), "sum", shape((half, share, 10 * block), BF), [VMEM], []
    )(partial)

    def back(first, ins, **more):
        return call(
            functools.partial(back_body, first, bands),
            "back",
            shape(frames_in.shape, BF),
            ins,
            [
                pltpu.VMEM((2, 4, wide + 2 * PAD, lanes), F32),
                pltpu.VMEM((3, 2, 4, wide, lanes), BF),
                pltpu.VMEM((2, 2, wide, lanes), BF),
                pltpu.SemaphoreType.DMA,
            ],
            flops=cells * lanes * lanes * 9,
            moved=2 << 20,
            to=HBM,
            **more,
        )

    through = feedthrough.reshape(1, lanes)
    grad_frames = back(0, [VMEM] * 4)(drive, kernel, cotangent, through)
    grad_frames = back(2, [VMEM] * 5 + [HBM], alias={5: 0})(
        drive, below, kernel, cotangent, through, grad_frames
    )
    whole = lax.all_to_all(partial, "tm", 0, 0, axis_index_groups=groups)
    whole, grad_frames = lax.optimization_barrier((whole, grad_frames))
    other = lax.ppermute(whole, "tm", swap)
    grad_kernel, grad_readout = call(
        last_body, "last", (shape((9, block, lanes), F32), shape((block, lanes), F32)), [VMEM] * 2, []
    )(whole, other)
    return grad_frames, grad_kernel, grad_readout.T


def solution(mesh):
    placed = (
        P("tm", "row", None, None),
        P("tm", "row", None, None),
        P(),
        P(),
        P(),
        P("tm", None),
        P("row", None, None),
    )
    return jax.shard_map(
        local,
        mesh=mesh,
        in_specs=placed,
        out_specs=(P("tm", "row", None, None), P(None, "row", None), P(None, "row")),
        check_vma=False,
    )
```

```python
import functools
import math

import jax
import jax.numpy as jnp
from jax import lax
from jax.experimental import pallas as pl
from jax.experimental.pallas import tpu as pltpu
from jax.sharding import PartitionSpec as P

SQRT_TWO_PI = 0.7978845608
CUBIC = 0.044715
BF = jnp.bfloat16
F32 = jnp.float32
PAD = 8
CELLS = ((0, 0), (0, 1), (1, 0), (1, 1), (2, 0), (2, 1), (3, 0), (3, 1))
VMEM = pl.BlockSpec(memory_space=pltpu.VMEM)
HBM = pl.BlockSpec(memory_space=pltpu.MemorySpace.HBM)


def call(body, outs, ins, scratch, flops=1 << 20, moved=1 << 20, grant=40 << 20, to=None, alias=None):
    many = isinstance(outs, (list, tuple))
    return pl.pallas_call(
        body,
        out_shape=outs,
        in_specs=ins,
        out_specs=[VMEM] * len(outs) if many else (to or VMEM),
        input_output_aliases=alias or {},
        scratch_shapes=scratch,
        cost_estimate=pl.CostEstimate(flops=flops, bytes_accessed=moved, transcendentals=0),
        compiler_params=pltpu.CompilerParams(vmem_limit_bytes=grant),
    )


def split3(value):
    high = value.astype(BF).astype(F32)
    rest = value - high
    middle = rest.astype(BF).astype(F32)
    return high, middle, rest - middle


def sublane(shape):
    return lax.broadcasted_iota(jnp.int32, shape, len(shape) - 2)


def gelu_slope(mixture):
    inside = SQRT_TWO_PI * (mixture + CUBIC * mixture * mixture * mixture)
    tangent = jnp.tanh(inside)
    return 0.5 * (1.0 + tangent) + 0.5 * mixture * (1.0 - tangent * tangent) * SQRT_TWO_PI * (
        1.0 + 3.0 * CUBIC * mixture * mixture
    )


def halo_body(frames, cotangent, start, out, begin, rows, slopes, starts, sems):
    wide = frames.shape[2]
    mine = lax.axis_index("tm")
    group = pl.multiple_of(8 * (mine // 4), 8)
    copies = (
        pltpu.make_async_copy(start.at[:, pl.ds(group, 8)], starts, sems.at[0]),
        pltpu.make_async_copy(frames.at[:, 2:4], rows, sems.at[1]),
        pltpu.make_async_copy(cotangent.at[:, 3], slopes, sems.at[2]),
    )
    for copy in copies:
        copy.start()
    for copy in copies:
        copy.wait()
    for f in range(2):
        for row in range(2):
            out[pl.ds((2 * f + row) * wide, wide), :] = rows[f, row]
        out[pl.ds((4 + f) * wide, wide), :] = slopes[f]
    offset = 2 * (mine % 4)
    step = sublane(begin.shape)
    total = jnp.zeros(begin.shape, F32)
    for place, row in ((2, 0), (4, 1), (6, 2)):
        moved = pltpu.roll(starts[row], (8 + place - offset) % 8, 0)
        total = jnp.where((step >= place) & (step < place + 2), moved, total)
    begin[...] = total
    pieces = split3(pltpu.roll(starts[3], (8 - offset) % 8, 0))
    total = jnp.where(step < 2, pieces[0], 0.0)
    total = jnp.where((step >= 2) & (step < 4), pltpu.roll(pieces[1], 2, 0), total)
    total = jnp.where((step >= 4) & (step < 6), pltpu.roll(pieces[2], 4, 0), total)
    out[pl.ds(6 * wide, 8), :] = total.astype(BF)


def places(pair, chips):
    return [(chip, pair - 2 * chip) for chip in range(chips) if 0 <= pair - 2 * chip <= 2]


def own_body(frames, cotangent, decay, out, grid, slopes, rows, given, rates, parts, sems):
    wide, lanes = frames.shape[2:]
    chips = out.shape[0]
    copies = (
        pltpu.make_async_copy(frames, rows, sems.at[0]),
        pltpu.make_async_copy(cotangent, given, sems.at[1]),
        pltpu.make_async_copy(decay, rates, sems.at[2]),
    )
    for copy in copies:
        copy.start()
    for f in range(2):
        for row in range(4):
            grid[f, row, 0:PAD, :] = jnp.zeros((PAD, lanes), F32)
            grid[f, row, PAD + wide :, :] = jnp.zeros((PAD, lanes), F32)
    for copy in copies:
        copy.wait()
    for f in range(2):
        for row in range(4):
            grid[f, row, PAD : PAD + wide, :] = rows[f, row].astype(F32)
        for row in range(3):
            slopes[f, row, PAD : PAD + wide, :] = given[f, row].astype(F32)
    for place, piece in enumerate(split3(rates[...])):
        parts[2 * place : 2 * place + 2, :] = piece
    parts[6:8, :] = jnp.zeros((2, lanes), F32)
    step = sublane((8, lanes))

    def stack(f, terms, first):
        block = None
        for place, row in terms:
            value = grid[f, row, first - place : first - place + 8, :]
            block = value if block is None else jnp.where(step < place, block, value)
        return block.astype(BF)

    for pair in range(wide // 2 + 1):
        first = PAD + 2 * pair - 1
        blocks = (
            stack(0, ((4, 0), (6, 1)), first),
            stack(0, ((0, 2), (2, 3)), first),
            stack(1, ((0, 0), (2, 1), (4, 2), (6, 3)), first),
        )
        for chip, place in places(pair, chips):
            for group in range(3):
                out[chip, 24 * place + 8 * group : 24 * place + 8 * group + 8, :] = blocks[group]
    for target in range(wide // 2):
        first = PAD + 2 * target
        for f in range(2):
            block = slopes[f, 0, first - 2 : first + 6, :]
            for place, row in ((4, 1), (6, 2)):
                block = jnp.where(step < place, block, slopes[f, row, first - place : first - place + 8, :])
            row = 72 + 16 * (target % 2) + 8 * f
            out[target // 2, row : row + 8, :] = block.astype(BF)
    for chip in range(chips):
        out[chip, 104:112, :] = parts[...].astype(BF)


def spread_body(own, halo, out, grid, slopes):
    wide = (halo.shape[0] - 8) // 6
    lanes = halo.shape[1]
    chips = out.shape[0]
    for f in range(2):
        for row in range(2):
            grid[f, row, 0:PAD, :] = jnp.zeros((PAD, lanes), F32)
            grid[f, row, PAD + wide :, :] = jnp.zeros((PAD, lanes), F32)
            grid[f, row, PAD : PAD + wide, :] = halo[pl.ds((2 * f + row) * wide, wide), :].astype(F32)
        slopes[f, PAD : PAD + wide, :] = halo[pl.ds((4 + f) * wide, wide), :].astype(F32)
    step = sublane((8, lanes))
    for pair in range(wide // 2 + 1):
        first = PAD + 2 * pair - 1
        upper = jnp.where(step < 2, grid[0, 0, first : first + 8, :], grid[0, 1, first - 2 : first + 6, :])
        lower = jnp.where(step < 6, grid[1, 0, first - 4 : first + 4, :], grid[1, 1, first - 6 : first + 2, :])
        for chip, place in places(pair, chips):
            row = 24 * place
            block = jnp.where(step < 4, upper, own[chip, row : row + 8, :].astype(F32))
            out[chip, row : row + 8, :] = block.astype(BF)
            block = jnp.where(step < 4, own[chip, row + 8 : row + 16, :].astype(F32), lower)
            out[chip, row + 8 : row + 16, :] = block.astype(BF)
            out[chip, row + 16 : row + 24, :] = own[chip, row + 16 : row + 24, :]
    for target in range(wide // 2):
        first = PAD + 2 * target
        for f in range(2):
            row = 72 + 16 * (target % 2) + 8 * f
            block = own[target // 2, row : row + 8, :].astype(F32)
            block = jnp.where(step < 2, slopes[f, first : first + 8, :], block)
            out[target // 2, row : row + 8, :] = block.astype(BF)
    for chip in range(chips):
        out[chip, 104:112, :] = own[chip, 104:112, :]


def cell_body(
    mine,
    theirs,
    kernel,
    readout,
    start,
    halo,
    give,
    keep,
    stay,
    grid,
    upstream,
    decay,
    gain,
    taps,
    driven,
    states,
    slopes,
    drive,
    turned,
):
    sources = 2 * mine.shape[0]
    count = sources * 16
    wide = (halo.shape[0] - 8) // 6
    lanes = mine.shape[2]
    core = lax.axis_index("tm") % 2
    step = sublane((8, lanes))
    is_first = lax.axis_index("row") == 0
    low = jnp.where(is_first & (step < 2), 0.0, 1.0)
    high = jnp.where(is_first & (step >= 2) & (step < 4), 0.0, 1.0)
    is_left = (step % 2) == 0

    def unpack(chip, _):
        for buffer, other in ((mine, core), (theirs, 1 - core)):
            source = 2 * chip + other
            for part in range(2):
                first = 24 * core + 24 * part
                group = [
                    buffer[chip, pl.ds(pl.multiple_of(first + 8 * g, 8), 8), :].astype(F32) for g in range(3)
                ]
                grid[2 * source, part, 8:16, :] = group[0]
                grid[2 * source, part, 16:24, :] = group[1]
                grid[2 * source + 1, part, 8:16, :] = group[1]
                grid[2 * source + 1, part, 16:24, :] = group[2]
            for f in range(2):
                first = pl.multiple_of(72 + 16 * core + 8 * f, 8)
                upstream[2 * source + f] = buffer[chip, pl.ds(first, 8), :].astype(F32)
            piece = buffer[chip, 104:112, :].astype(F32)
            rate = piece + pltpu.roll(piece, 6, 0) + pltpu.roll(piece, 4, 0)
            decay[source] = rate
            gain[source] = jnp.sqrt(1.0 - rate * rate)
        return _

    lax.fori_loop(0, sources // 2, unpack, 0, unroll=2)

    def gather(source, _):
        rows = pl.ds(pl.multiple_of(16 * source, 16), 16)
        for i in range(3):
            for j in range(3):
                pair = []
                for f in range(2):
                    frame = 2 * source + f
                    first = 8 + 4 * f + 2 * i
                    if j == 1:
                        value = jnp.where(
                            is_left,
                            grid[frame, 0, first + 1 : first + 9, :],
                            grid[frame, 1, first - 1 : first + 7, :],
                        )
                    else:
                        value = grid[frame, j // 2, first : first + 8, :]
                    if i == 2:
                        value = value * low
                    if i == 0:
                        value = value * high
                    pair.append(value)
                tap = 3 * i + j
                taps[rows, lanes * tap : lanes * tap + lanes] = jnp.concatenate(pair, axis=0).astype(BF)
        return _

    chunk = min(count, 128)
    for part in range(count // chunk):
        for source in range(chunk // 16):
            gather(part * (chunk // 16) + source, 0)
        rows = slice(part * chunk, part * chunk + chunk)
        driven[rows, :] = jnp.dot(taps[rows, :], kernel[...], preferred_element_type=F32)

    tail = halo[6 * wide : 6 * wide + 8, :].astype(F32)
    tail = tail + pltpu.roll(tail, 6, 0) + pltpu.roll(tail, 4, 0)
    begin = jnp.where(step < 2, tail, start[...])

    def advance(source, state):
        pair = []
        for f in range(2):
            rate = jnp.broadcast_to(decay[source, f : f + 1, :], state.shape)
            size = jnp.broadcast_to(gain[source, f : f + 1, :], state.shape)
            now = driven[pl.ds(pl.multiple_of(16 * source + 8 * f, 8), 8), :]
            state = rate * state + size * now
            pair.append(state)
        states[pl.ds(pl.multiple_of(16 * source, 16), 16), :] = jnp.concatenate(pair, axis=0).astype(BF)
        return state

    lax.fori_loop(0, sources, advance, begin, unroll=4)

    def mix(part, _):
        rows = pl.ds(pl.multiple_of(part * 64, 64), 64)
        mixture = jnp.dot(states[rows, :], readout[...], preferred_element_type=F32)
        given = upstream[pl.ds(pl.multiple_of(part * 8, 8), 8)].reshape(64, lanes)
        slope = (given * gelu_slope(mixture)).astype(BF)
        slopes[rows, :] = slope
        driven[rows, :] = lax.dot_general(
            slope, readout[...], (((1,), (1,)), ((), ())), preferred_element_type=F32
        )
        return _

    lax.fori_loop(0, count // 64, mix, 0, unroll=8)

    def retreat(turn, carried):
        adjoint, later = carried
        source = sources - 1 - turn
        pair = []
        for f in (1, 0):
            now = driven[pl.ds(pl.multiple_of(16 * source + 8 * f, 8), 8), :]
            adjoint = now + later * adjoint
            later = jnp.broadcast_to(decay[source, f : f + 1, :], adjoint.shape)
            value = jnp.broadcast_to(gain[source, f : f + 1, :], adjoint.shape) * adjoint
            pair.append(value)
        drive[pl.ds(pl.multiple_of(16 * source, 16), 16), :] = jnp.concatenate(pair[::-1], axis=0)
        return adjoint, later

    nothing = jnp.zeros((8, lanes), F32)
    lax.fori_loop(0, sources, retreat, (nothing, nothing), unroll=4)

    half = sources // 2
    share = lanes // sources
    is_even = lax.axis_index("tm") % 2 == 0

    def partners_first(value):
        blocks = value.astype(F32).reshape(half, 2, share, count)
        even, odd = blocks[:, 0].reshape(lanes // 2, count), blocks[:, 1].reshape(lanes // 2, count)
        order = (jnp.where(is_even, odd, even), jnp.where(is_even, even, odd))
        return jnp.concatenate(order, axis=0).astype(BF)

    for chip in range(half):
        for f in range(2):
            even = drive[32 * chip + 8 * f : 32 * chip + 8 * f + 8, :]
            odd = drive[32 * chip + 8 * f + 16 : 32 * chip + 8 * f + 24, :]
            columns = slice(10 * lanes + f * lanes, 11 * lanes + f * lanes)
            give[chip, 0:8, columns] = jnp.where(is_even, odd, even).astype(BF)
            stay[chip, :, f * lanes : f * lanes + lanes] = jnp.where(is_even, even, odd).astype(BF)
    turned[...] = partners_first(drive[...].astype(BF).T)
    for tap in range(9):
        columns = slice(lanes * tap, lanes * tap + lanes)
        term = jnp.dot(turned[...], taps[:, columns], preferred_element_type=F32)
        give[:, :, columns] = term[: lanes // 2].astype(BF).reshape(half, share, lanes)
        keep[:, :, columns] = term[lanes // 2 :].reshape(half, share, lanes)
    turned[...] = partners_first(states[...].T)
    columns = slice(9 * lanes, 10 * lanes)
    term = jnp.dot(turned[...], slopes[...], preferred_element_type=F32)
    give[:, :, columns] = term[: lanes // 2].astype(BF).reshape(half, share, lanes)
    keep[:, :, columns] = term[lanes // 2 :].reshape(half, share, lanes)


def merge_body(taken, keep, stay, out):
    lanes = stay.shape[2] // 2
    for chip in range(out.shape[0]):
        total = keep[chip] + taken[chip, :, : 10 * lanes].astype(F32)
        out[chip, :, : 10 * lanes] = total.astype(BF)
    is_even = lax.axis_index("tm") % 2 == 0

    @pl.when(is_even)
    def _():
        out[:, 0:8, 10 * lanes : 12 * lanes] = stay[...]
        out[:, 0:8, 12 * lanes : 14 * lanes] = taken[:, 0:8, 10 * lanes : 12 * lanes]

    @pl.when(jnp.logical_not(is_even))
    def _():
        out[:, 0:8, 10 * lanes : 12 * lanes] = taken[:, 0:8, 10 * lanes : 12 * lanes]
        out[:, 0:8, 12 * lanes : 14 * lanes] = stay[...]


def join_body(bands, got, total, frames, top, cells, grid):
    chips, share, width = got.shape
    sources = 2 * chips
    lanes = width // 14

    def add(source, carried):
        return carried + got[source, :, : 10 * lanes].astype(F32)

    sums = lax.fori_loop(0, chips, add, jnp.zeros((share, 10 * lanes), F32), unroll=2)
    block = lanes // bands
    for band in range(bands):
        total[band] = jnp.concatenate(
            [sums[:, lanes * k + block * band : lanes * k + block * band + block] for k in range(10)], axis=1
        ).astype(BF)

    for f in range(2):
        for part in range(lanes // 128):
            for source in range(sources):
                first = (10 + f + 2 * (source % 2)) * lanes + 128 * part
                cells[8 * source : 8 * source + 8, :] = got[source // 2, 0:8, first : first + 128].astype(F32)
            for place, (row, column) in enumerate(CELLS):
                grid[pl.ds(column, sources, stride=2), :] = cells[pl.ds(place, sources, stride=8), :]
                if column == 1:
                    value = grid[...].astype(BF)
                    frames[f, row, :, 128 * part : 128 * part + 128] = value
                    if row < 2:
                        top[f, row, :, 128 * part : 128 * part + 128] = value


def back_body(first, bands, *refs):
    if first:
        drive, below, kernel, cotangent, feedthrough, _, out, grid, moved, done, sem = refs
    else:
        drive, kernel, cotangent, feedthrough, out, grid, moved, done, sem = refs
    wide, lanes = drive.shape[2:]
    band = lax.axis_index("row")
    for row in range(first, first + 4):
        keep = None
        if row == 0:
            keep = jnp.where(band == 0, 0.0, 1.0)
        if row == 5:
            keep = jnp.where(band == bands - 1, 0.0, 1.0)
        for f in range(2):
            source = (drive[f, row] if row < 4 else below[f, row - 4]).astype(F32)
            if keep is not None:
                source = source * keep
            grid[f, row - first, 0:PAD, :] = jnp.zeros((PAD, lanes), F32)
            grid[f, row - first, PAD + wide :, :] = jnp.zeros((PAD, lanes), F32)
            grid[f, row - first, PAD : PAD + wide, :] = source
            for shift in range(3):
                begin = PAD - 1 + shift
                moved[shift, f, row - first] = grid[f, row - first, begin : begin + wide, :].astype(BF)
    for f in range(2):
        total = jnp.zeros((2 * wide, lanes), F32)
        for i in range(3):
            for j in range(3):
                cells = moved[2 - j, f, 2 - i : 4 - i].reshape(2 * wide, lanes)
                total = total + lax.dot_general(
                    cells, kernel[3 * i + j], (((1,), (1,)), ((), ())), preferred_element_type=F32
                )
        given = cotangent[f, first : first + 2].astype(F32).reshape(2 * wide, lanes)
        done[f] = (total + feedthrough[...] * given).astype(BF).reshape(2, wide, lanes)
    store = pltpu.make_async_copy(done, out.at[:, first : first + 2], sem)
    store.start()
    store.wait()


def sum_body(scaling, got, out):
    total = got[0].astype(F32)
    for band in range(1, got.shape[0]):
        total = total + got[band].astype(F32)
    total = (total * scaling).astype(BF)
    for target in range(out.shape[0]):
        out[target] = total


def last_body(got, kernel_out, readout_out):
    sources, share, width = got.shape
    turned = got[...].astype(F32).reshape(sources * share, width).T
    block = width // 10
    for k in range(9):
        kernel_out[k] = turned[block * k : block * k + block]
    readout_out[...] = turned[9 * block :]


def local(frames_in, cotangent, kernel, readout, feedthrough, decay_rate, start_state):
    here, band_rows, wide, lanes = frames_in.shape
    sources, bands = lax.axis_size("tm"), lax.axis_size("row")
    cells = sources * 16
    share = lanes // sources
    block = lanes // bands
    shape = jax.ShapeDtypeStruct
    down = [(i, (i + 1) % bands) for i in range(bands)]
    up = [((i + 1) % bands, i) for i in range(bands)]

    edge, begin = call(
        halo_body,
        (shape((6 * wide + 8, lanes), BF), shape((8, lanes), F32)),
        [HBM] * 3,
        [
            pltpu.VMEM((2, 2, wide, lanes), BF),
            pltpu.VMEM((2, wide, lanes), BF),
            pltpu.VMEM((4, 8, lanes), F32),
            pltpu.SemaphoreType.DMA((3,)),
        ],
        grant=63 << 20,
    )(frames_in, cotangent, start_state)
    edge = lax.ppermute(edge, "row", down)
    half = sources // 2
    groups = [[2 * chip + core for chip in range(half)] for core in range(2)]
    swap = [(i, i ^ 1) for i in range(sources)]
    own = call(
        own_body,
        shape((half, 112, lanes), BF),
        [HBM] * 3,
        [
            pltpu.VMEM((2, 4, wide + 2 * PAD, lanes), F32),
            pltpu.VMEM((2, 3, wide + 2 * PAD, lanes), F32),
            pltpu.VMEM((2, 4, wide, lanes), BF),
            pltpu.VMEM((2, 4, wide, lanes), BF),
            pltpu.VMEM((2, lanes), F32),
            pltpu.VMEM((8, lanes), F32),
            pltpu.SemaphoreType.DMA((3,)),
        ],
        moved=8 << 20,
    )(frames_in, cotangent, decay_rate)
    send = call(
        spread_body,
        shape((half, 112, lanes), BF),
        [VMEM] * 2,
        [
            pltpu.VMEM((2, 2, wide + 2 * PAD, lanes), F32),
            pltpu.VMEM((2, wide + 2 * PAD, lanes), F32),
        ],
    )(own, edge)
    mine = lax.all_to_all(send, "tm", 0, 0, axis_index_groups=groups)
    theirs = lax.ppermute(mine, "tm", swap)
    give, keep, stay = call(
        cell_body,
        (
            shape((half, share, 12 * lanes), BF),
            shape((half, share, 10 * lanes), F32),
            shape((half, 8, 2 * lanes), BF),
        ),
        [VMEM] * 6,
        [
            pltpu.VMEM((2 * sources, 2, 32, lanes), F32),
            pltpu.VMEM((2 * sources, 8, lanes), F32),
            pltpu.VMEM((sources, 8, lanes), F32),
            pltpu.VMEM((sources, 8, lanes), F32),
            pltpu.VMEM((cells, 9 * lanes), BF),
            pltpu.VMEM((cells, lanes), F32),
            pltpu.VMEM((cells, lanes), BF),
            pltpu.VMEM((cells, lanes), BF),
            pltpu.VMEM((cells, lanes), F32),
            pltpu.VMEM((lanes, cells), BF),
        ],
        flops=2 * cells * lanes * lanes * 21,
        moved=4 << 20,
    )(mine, theirs, kernel.reshape(9 * lanes, lanes), readout, begin, edge)
    taken = lax.ppermute(give, "tm", swap)
    send = call(merge_body, shape((half, share, 14 * lanes), BF), [VMEM] * 3, [])(taken, keep, stay)
    got = lax.all_to_all(send, "tm", 0, 0, axis_index_groups=groups)
    partial, drive, top = call(
        functools.partial(join_body, bands),
        (
            shape((bands, share, 10 * block), BF),
            shape((2, 4, wide, lanes), BF),
            shape((2, 2, wide, lanes), BF),
        ),
        [VMEM],
        [pltpu.VMEM((8 * sources, 128), F32), pltpu.VMEM((wide, 128), F32)],
    )(got)
    below = lax.ppermute(top, "row", up)
    partial = lax.all_to_all(partial, "row", 0, 0)
    scaling = 1.0 / math.sqrt(here * sources * band_rows * bands * wide)
    partial = call(functools.partial(sum_body, scaling), shape((sources, share, 10 * block), BF), [VMEM], [])(partial)

    def back(first, ins, **more):
        return call(
            functools.partial(back_body, first, bands),
            shape(frames_in.shape, BF),
            ins,
            [
                pltpu.VMEM((2, 4, wide + 2 * PAD, lanes), F32),
                pltpu.VMEM((3, 2, 4, wide, lanes), BF),
                pltpu.VMEM((2, 2, wide, lanes), BF),
                pltpu.SemaphoreType.DMA,
            ],
            flops=cells * lanes * lanes * 9,
            moved=2 << 20,
            to=HBM,
            **more,
        )

    through = feedthrough.reshape(1, lanes)
    grad_frames = back(0, [VMEM] * 4)(drive, kernel, cotangent, through)
    grad_frames = back(2, [VMEM] * 5 + [HBM], alias={5: 0})(
        drive, below, kernel, cotangent, through, grad_frames
    )
    whole = lax.all_to_all(partial, "tm", 0, 0)
    whole, grad_frames = lax.optimization_barrier((whole, grad_frames))
    grad_kernel, grad_readout = call(
        last_body, (shape((9, block, lanes), F32), shape((block, lanes), F32)), [VMEM], []
    )(whole)
    return grad_frames, grad_kernel, grad_readout.T


def solution(mesh):
    placed = (
        P("tm", "row", None, None),
        P("tm", "row", None, None),
        P(),
        P(),
        P(),
        P("tm", None),
        P("row", None, None),
    )

    return jax.shard_map(
        local,
        mesh=mesh,
        in_specs=placed,
        out_specs=(P("tm", "row", None, None), P(None, "row", None), P(None, "row")),
        check_vma=False,
    )
```

```python
import functools
import math

import jax
import jax.numpy as jnp
from jax import lax
from jax.experimental import pallas as pl
from jax.experimental.pallas import tpu as pltpu
from jax.sharding import PartitionSpec as P

SQRT_TWO_PI = 0.7978845608
CUBIC = 0.044715
BF = jnp.bfloat16
F32 = jnp.float32
PAD = 8
CELLS = ((0, 0), (0, 1), (1, 0), (1, 1), (2, 0), (2, 1), (3, 0), (3, 1))
VMEM = pl.BlockSpec(memory_space=pltpu.VMEM)
HBM = pl.BlockSpec(memory_space=pltpu.MemorySpace.HBM)


def call(body, name, outs, ins, scratch, flops=1 << 20, moved=1 << 20, grant=40 << 20, to=None, alias=None):
    many = isinstance(outs, (list, tuple))
    return pl.pallas_call(
        body,
        name=name,
        out_shape=outs,
        in_specs=ins,
        out_specs=[VMEM] * len(outs) if many else (to or VMEM),
        input_output_aliases=alias or {},
        scratch_shapes=scratch,
        cost_estimate=pl.CostEstimate(flops=flops, bytes_accessed=moved, transcendentals=0),
        compiler_params=pltpu.CompilerParams(vmem_limit_bytes=grant),
    )


def split3(value):
    high = value.astype(BF).astype(F32)
    rest = value - high
    middle = rest.astype(BF).astype(F32)
    return high, middle, rest - middle


def sublane(shape):
    return lax.broadcasted_iota(jnp.int32, shape, len(shape) - 2)


def gelu_slope(mixture):
    inside = SQRT_TWO_PI * (mixture + CUBIC * mixture * mixture * mixture)
    tangent = jnp.tanh(inside)
    return 0.5 * (1.0 + tangent) + 0.5 * mixture * (1.0 - tangent * tangent) * SQRT_TWO_PI * (
        1.0 + 3.0 * CUBIC * mixture * mixture
    )


def halo_body(frames, cotangent, start, out, begin, rows, slopes, starts, sems):
    wide = frames.shape[2]
    mine = lax.axis_index("tm")
    group = pl.multiple_of(8 * (mine // 4), 8)
    copies = (
        pltpu.make_async_copy(start.at[:, pl.ds(group, 8)], starts, sems.at[0]),
        pltpu.make_async_copy(frames.at[:, 2:4], rows, sems.at[1]),
        pltpu.make_async_copy(cotangent.at[:, 3], slopes, sems.at[2]),
    )
    for copy in copies:
        copy.start()
    for copy in copies:
        copy.wait()
    for f in range(2):
        for row in range(2):
            out[pl.ds((2 * f + row) * wide, wide), :] = rows[f, row]
        out[pl.ds((4 + f) * wide, wide), :] = slopes[f]
    offset = 2 * (mine % 4)
    step = sublane(begin.shape)
    total = jnp.zeros(begin.shape, F32)
    for place, row in ((2, 0), (4, 1), (6, 2)):
        moved = pltpu.roll(starts[row], (8 + place - offset) % 8, 0)
        total = jnp.where((step >= place) & (step < place + 2), moved, total)
    begin[...] = total
    pieces = split3(pltpu.roll(starts[3], (8 - offset) % 8, 0))
    total = jnp.where(step < 2, pieces[0], 0.0)
    total = jnp.where((step >= 2) & (step < 4), pltpu.roll(pieces[1], 2, 0), total)
    total = jnp.where((step >= 4) & (step < 6), pltpu.roll(pieces[2], 4, 0), total)
    out[pl.ds(6 * wide, 8), :] = total.astype(BF)


def places(pair, chips):
    return [(chip, pair - 2 * chip) for chip in range(chips) if 0 <= pair - 2 * chip <= 2]


def own_body(frames, cotangent, decay, out, grid, slopes, rows, given, rates, parts, sems):
    wide, lanes = frames.shape[2:]
    chips = out.shape[0]
    copies = (
        pltpu.make_async_copy(frames, rows, sems.at[0]),
        pltpu.make_async_copy(cotangent, given, sems.at[1]),
        pltpu.make_async_copy(decay, rates, sems.at[2]),
    )
    for copy in copies:
        copy.start()
    for f in range(2):
        for row in range(4):
            grid[f, row, 0:PAD, :] = jnp.zeros((PAD, lanes), F32)
            grid[f, row, PAD + wide :, :] = jnp.zeros((PAD, lanes), F32)
    for copy in copies:
        copy.wait()
    for f in range(2):
        for row in range(4):
            grid[f, row, PAD : PAD + wide, :] = rows[f, row].astype(F32)
        for row in range(3):
            slopes[f, row, PAD : PAD + wide, :] = given[f, row].astype(F32)
    for place, piece in enumerate(split3(rates[...])):
        parts[2 * place : 2 * place + 2, :] = piece
    parts[6:8, :] = jnp.zeros((2, lanes), F32)
    step = sublane((8, lanes))

    def stack(f, terms, first):
        block = None
        for place, row in terms:
            value = grid[f, row, first - place : first - place + 8, :]
            block = value if block is None else jnp.where(step < place, block, value)
        return block.astype(BF)

    for pair in range(wide // 2 + 1):
        first = PAD + 2 * pair - 1
        blocks = (
            stack(0, ((4, 0), (6, 1)), first),
            stack(0, ((0, 2), (2, 3)), first),
            stack(1, ((0, 0), (2, 1), (4, 2), (6, 3)), first),
        )
        for chip, place in places(pair, chips):
            for group in range(3):
                out[chip, 24 * place + 8 * group : 24 * place + 8 * group + 8, :] = blocks[group]
    for target in range(wide // 2):
        first = PAD + 2 * target
        for f in range(2):
            block = slopes[f, 0, first - 2 : first + 6, :]
            for place, row in ((4, 1), (6, 2)):
                block = jnp.where(step < place, block, slopes[f, row, first - place : first - place + 8, :])
            row = 72 + 16 * (target % 2) + 8 * f
            out[target // 2, row : row + 8, :] = block.astype(BF)
    for chip in range(chips):
        out[chip, 104:112, :] = parts[...].astype(BF)


def spread_body(own, halo, out, grid, slopes):
    wide = (halo.shape[0] - 8) // 6
    lanes = halo.shape[1]
    chips = out.shape[0]
    for f in range(2):
        for row in range(2):
            grid[f, row, 0:PAD, :] = jnp.zeros((PAD, lanes), F32)
            grid[f, row, PAD + wide :, :] = jnp.zeros((PAD, lanes), F32)
            grid[f, row, PAD : PAD + wide, :] = halo[pl.ds((2 * f + row) * wide, wide), :].astype(F32)
        slopes[f, PAD : PAD + wide, :] = halo[pl.ds((4 + f) * wide, wide), :].astype(F32)
    step = sublane((8, lanes))
    for pair in range(wide // 2 + 1):
        first = PAD + 2 * pair - 1
        upper = jnp.where(step < 2, grid[0, 0, first : first + 8, :], grid[0, 1, first - 2 : first + 6, :])
        lower = jnp.where(step < 6, grid[1, 0, first - 4 : first + 4, :], grid[1, 1, first - 6 : first + 2, :])
        for chip, place in places(pair, chips):
            row = 24 * place
            block = jnp.where(step < 4, upper, own[chip, row : row + 8, :].astype(F32))
            out[chip, row : row + 8, :] = block.astype(BF)
            block = jnp.where(step < 4, own[chip, row + 8 : row + 16, :].astype(F32), lower)
            out[chip, row + 8 : row + 16, :] = block.astype(BF)
            out[chip, row + 16 : row + 24, :] = own[chip, row + 16 : row + 24, :]
    for target in range(wide // 2):
        first = PAD + 2 * target
        for f in range(2):
            row = 72 + 16 * (target % 2) + 8 * f
            block = own[target // 2, row : row + 8, :].astype(F32)
            block = jnp.where(step < 2, slopes[f, first : first + 8, :], block)
            out[target // 2, row : row + 8, :] = block.astype(BF)
    for chip in range(chips):
        out[chip, 104:112, :] = own[chip, 104:112, :]


def cell_body(
    mine,
    theirs,
    kernel,
    readout,
    start,
    halo,
    give,
    keep,
    stay,
    grid,
    upstream,
    decay,
    gain,
    taps,
    driven,
    states,
    slopes,
    drive,
    turned,
):
    sources = 2 * mine.shape[0]
    count = sources * 16
    wide = (halo.shape[0] - 8) // 6
    lanes = mine.shape[2]
    core = lax.axis_index("tm") % 2
    step = sublane((8, lanes))
    is_first = lax.axis_index("row") == 0
    low = jnp.where(is_first & (step < 2), 0.0, 1.0)
    high = jnp.where(is_first & (step >= 2) & (step < 4), 0.0, 1.0)
    is_left = (step % 2) == 0

    def unpack(chip, _):
        for buffer, other in ((mine, core), (theirs, 1 - core)):
            source = 2 * chip + other
            for part in range(2):
                first = 24 * core + 24 * part
                group = [
                    buffer[chip, pl.ds(pl.multiple_of(first + 8 * g, 8), 8), :].astype(F32) for g in range(3)
                ]
                grid[2 * source, part, 8:16, :] = group[0]
                grid[2 * source, part, 16:24, :] = group[1]
                grid[2 * source + 1, part, 8:16, :] = group[1]
                grid[2 * source + 1, part, 16:24, :] = group[2]
            for f in range(2):
                first = pl.multiple_of(72 + 16 * core + 8 * f, 8)
                upstream[2 * source + f] = buffer[chip, pl.ds(first, 8), :].astype(F32)
            piece = buffer[chip, 104:112, :].astype(F32)
            rate = piece + pltpu.roll(piece, 6, 0) + pltpu.roll(piece, 4, 0)
            decay[source] = rate
            gain[source] = jnp.sqrt(1.0 - rate * rate)
        return _

    lax.fori_loop(0, sources // 2, unpack, 0, unroll=4)

    def gather(source, _):
        rows = pl.ds(pl.multiple_of(16 * source, 16), 16)
        for i in range(3):
            for j in range(3):
                pair = []
                for f in range(2):
                    frame = 2 * source + f
                    first = 8 + 4 * f + 2 * i
                    if j == 1:
                        value = jnp.where(
                            is_left,
                            grid[frame, 0, first + 1 : first + 9, :],
                            grid[frame, 1, first - 1 : first + 7, :],
                        )
                    else:
                        value = grid[frame, j // 2, first : first + 8, :]
                    if i == 2:
                        value = value * low
                    if i == 0:
                        value = value * high
                    pair.append(value)
                tap = 3 * i + j
                taps[rows, lanes * tap : lanes * tap + lanes] = jnp.concatenate(pair, axis=0).astype(BF)
        return _

    chunk = min(count, 128)
    for part in range(count // chunk):
        for source in range(chunk // 16):
            gather(part * (chunk // 16) + source, 0)
        rows = slice(part * chunk, part * chunk + chunk)
        driven[rows, :] = jnp.dot(taps[rows, :], kernel[...], preferred_element_type=F32)

    tail = halo[6 * wide : 6 * wide + 8, :].astype(F32)
    tail = tail + pltpu.roll(tail, 6, 0) + pltpu.roll(tail, 4, 0)
    begin = jnp.where(step < 2, tail, start[...])

    def advance(source, state):
        pair = []
        for f in range(2):
            rate = jnp.broadcast_to(decay[source, f : f + 1, :], state.shape)
            size = jnp.broadcast_to(gain[source, f : f + 1, :], state.shape)
            now = driven[pl.ds(pl.multiple_of(16 * source + 8 * f, 8), 8), :]
            state = rate * state + size * now
            pair.append(state)
        states[pl.ds(pl.multiple_of(16 * source, 16), 16), :] = jnp.concatenate(pair, axis=0).astype(BF)
        return state

    lax.fori_loop(0, sources, advance, begin, unroll=8)

    def mix(part, _):
        rows = pl.ds(pl.multiple_of(part * 64, 64), 64)
        mixture = jnp.dot(states[rows, :], readout[...], preferred_element_type=F32)
        given = upstream[pl.ds(pl.multiple_of(part * 8, 8), 8)].reshape(64, lanes)
        slope = (given * gelu_slope(mixture)).astype(BF)
        slopes[rows, :] = slope
        driven[rows, :] = lax.dot_general(
            slope, readout[...], (((1,), (1,)), ((), ())), preferred_element_type=F32
        )
        return _

    lax.fori_loop(0, count // 64, mix, 0, unroll=8)

    def retreat(turn, carried):
        adjoint, later = carried
        source = sources - 1 - turn
        pair = []
        for f in (1, 0):
            now = driven[pl.ds(pl.multiple_of(16 * source + 8 * f, 8), 8), :]
            adjoint = now + later * adjoint
            later = jnp.broadcast_to(decay[source, f : f + 1, :], adjoint.shape)
            value = jnp.broadcast_to(gain[source, f : f + 1, :], adjoint.shape) * adjoint
            pair.append(value)
        drive[pl.ds(pl.multiple_of(16 * source, 16), 16), :] = jnp.concatenate(pair[::-1], axis=0)
        return adjoint, later

    nothing = jnp.zeros((8, lanes), F32)
    lax.fori_loop(0, sources, retreat, (nothing, nothing), unroll=8)

    half = sources // 2
    share = lanes // sources
    is_even = lax.axis_index("tm") % 2 == 0

    def partners_first(value):
        blocks = value.astype(F32).reshape(half, 2, share, count)
        even, odd = blocks[:, 0].reshape(lanes // 2, count), blocks[:, 1].reshape(lanes // 2, count)
        order = (jnp.where(is_even, odd, even), jnp.where(is_even, even, odd))
        return jnp.concatenate(order, axis=0).astype(BF)

    for chip in range(half):
        for f in range(2):
            even = drive[32 * chip + 8 * f : 32 * chip + 8 * f + 8, :]
            odd = drive[32 * chip + 8 * f + 16 : 32 * chip + 8 * f + 24, :]
            columns = slice(10 * lanes + f * lanes, 11 * lanes + f * lanes)
            give[chip, 0:8, columns] = jnp.where(is_even, odd, even).astype(BF)
            stay[chip, :, f * lanes : f * lanes + lanes] = jnp.where(is_even, even, odd).astype(BF)
    turned[...] = partners_first(drive[...].astype(BF).T)
    for tap in range(9):
        columns = slice(lanes * tap, lanes * tap + lanes)
        term = jnp.dot(turned[...], taps[:, columns], preferred_element_type=F32)
        give[:, :, columns] = term[: lanes // 2].astype(BF).reshape(half, share, lanes)
        keep[:, :, columns] = term[lanes // 2 :].reshape(half, share, lanes)
    turned[...] = partners_first(states[...].T)
    columns = slice(9 * lanes, 10 * lanes)
    term = jnp.dot(turned[...], slopes[...], preferred_element_type=F32)
    give[:, :, columns] = term[: lanes // 2].astype(BF).reshape(half, share, lanes)
    keep[:, :, columns] = term[lanes // 2 :].reshape(half, share, lanes)


def merge_body(taken, keep, stay, out):
    lanes = stay.shape[2] // 2
    for chip in range(out.shape[0]):
        total = keep[chip] + taken[chip, :, : 10 * lanes].astype(F32)
        out[chip, :, : 10 * lanes] = total.astype(BF)
    is_even = lax.axis_index("tm") % 2 == 0

    @pl.when(is_even)
    def _():
        out[:, 0:8, 10 * lanes : 12 * lanes] = stay[...]
        out[:, 0:8, 12 * lanes : 14 * lanes] = taken[:, 0:8, 10 * lanes : 12 * lanes]

    @pl.when(jnp.logical_not(is_even))
    def _():
        out[:, 0:8, 10 * lanes : 12 * lanes] = taken[:, 0:8, 10 * lanes : 12 * lanes]
        out[:, 0:8, 12 * lanes : 14 * lanes] = stay[...]


def join_body(bands, got, total, frames, top, cells, grid):
    chips, share, width = got.shape
    sources = 2 * chips
    lanes = width // 14

    def add(source, carried):
        return carried + got[source, :, : 10 * lanes].astype(F32)

    sums = lax.fori_loop(0, chips, add, jnp.zeros((share, 10 * lanes), F32), unroll=2)
    block = lanes // bands
    for band in range(bands):
        total[band] = jnp.concatenate(
            [sums[:, lanes * k + block * band : lanes * k + block * band + block] for k in range(10)], axis=1
        ).astype(BF)

    for f in range(2):
        for part in range(lanes // 128):
            for source in range(sources):
                first = (10 + f + 2 * (source % 2)) * lanes + 128 * part
                cells[8 * source : 8 * source + 8, :] = got[source // 2, 0:8, first : first + 128].astype(F32)
            for place, (row, column) in enumerate(CELLS):
                grid[pl.ds(column, sources, stride=2), :] = cells[pl.ds(place, sources, stride=8), :]
                if column == 1:
                    value = grid[...].astype(BF)
                    frames[f, row, :, 128 * part : 128 * part + 128] = value
                    if row < 2:
                        top[f, row, :, 128 * part : 128 * part + 128] = value


def back_body(first, bands, *refs):
    if first:
        drive, below, kernel, cotangent, feedthrough, _, out, grid, moved, done, sem = refs
    else:
        drive, kernel, cotangent, feedthrough, out, grid, moved, done, sem = refs
    wide, lanes = drive.shape[2:]
    band = lax.axis_index("row")
    for row in range(first, first + 4):
        keep = None
        if row == 0:
            keep = jnp.where(band == 0, 0.0, 1.0)
        if row == 5:
            keep = jnp.where(band == bands - 1, 0.0, 1.0)
        for f in range(2):
            source = (drive[f, row] if row < 4 else below[f, row - 4]).astype(F32)
            if keep is not None:
                source = source * keep
            grid[f, row - first, 0:PAD, :] = jnp.zeros((PAD, lanes), F32)
            grid[f, row - first, PAD + wide :, :] = jnp.zeros((PAD, lanes), F32)
            grid[f, row - first, PAD : PAD + wide, :] = source
            for shift in range(3):
                begin = PAD - 1 + shift
                moved[shift, f, row - first] = grid[f, row - first, begin : begin + wide, :].astype(BF)
    for f in range(2):
        total = jnp.zeros((2 * wide, lanes), F32)
        for i in range(3):
            for j in range(3):
                cells = moved[2 - j, f, 2 - i : 4 - i].reshape(2 * wide, lanes)
                total = total + lax.dot_general(
                    cells, kernel[3 * i + j], (((1,), (1,)), ((), ())), preferred_element_type=F32
                )
        given = cotangent[f, first : first + 2].astype(F32).reshape(2 * wide, lanes)
        done[f] = (total + feedthrough[...] * given).astype(BF).reshape(2, wide, lanes)
    store = pltpu.make_async_copy(done, out.at[:, first : first + 2], sem)
    store.start()
    store.wait()


def sum_body(scaling, got, out):
    total = got[0].astype(F32)
    for band in range(1, got.shape[0]):
        total = total + got[band].astype(F32)
    total = (total * scaling).astype(BF)
    for target in range(out.shape[0]):
        out[target] = total


def last_body(mine, theirs, kernel_out, readout_out):
    chips, share, width = mine.shape
    is_even = lax.axis_index("tm") % 2 == 0
    here, there = mine[...].astype(F32), theirs[...].astype(F32)
    pairs = [jnp.where(is_even, here, there), jnp.where(is_even, there, here)]
    turned = jnp.stack(pairs, axis=1).reshape(2 * chips * share, width).T
    block = width // 10
    for k in range(9):
        kernel_out[k] = turned[block * k : block * k + block]
    readout_out[...] = turned[9 * block :]


def local(frames_in, cotangent, kernel, readout, feedthrough, decay_rate, start_state):
    here, band_rows, wide, lanes = frames_in.shape
    sources, bands = lax.axis_size("tm"), lax.axis_size("row")
    cells = sources * 16
    share = lanes // sources
    block = lanes // bands
    shape = jax.ShapeDtypeStruct
    down = [(i, (i + 1) % bands) for i in range(bands)]
    up = [((i + 1) % bands, i) for i in range(bands)]

    edge, begin = call(
        halo_body,
        "halo",
        (shape((6 * wide + 8, lanes), BF), shape((8, lanes), F32)),
        [HBM] * 3,
        [
            pltpu.VMEM((2, 2, wide, lanes), BF),
            pltpu.VMEM((2, wide, lanes), BF),
            pltpu.VMEM((4, 8, lanes), F32),
            pltpu.SemaphoreType.DMA((3,)),
        ],
        grant=63 << 20,
    )(frames_in, cotangent, start_state)
    edge = lax.ppermute(edge, "row", down)
    half = sources // 2
    groups = [[2 * chip + core for chip in range(half)] for core in range(2)]
    swap = [(i, i ^ 1) for i in range(sources)]
    own = call(
        own_body,
        "own",
        shape((half, 112, lanes), BF),
        [HBM] * 3,
        [
            pltpu.VMEM((2, 4, wide + 2 * PAD, lanes), F32),
            pltpu.VMEM((2, 3, wide + 2 * PAD, lanes), F32),
            pltpu.VMEM((2, 4, wide, lanes), BF),
            pltpu.VMEM((2, 4, wide, lanes), BF),
            pltpu.VMEM((2, lanes), F32),
            pltpu.VMEM((8, lanes), F32),
            pltpu.SemaphoreType.DMA((3,)),
        ],
        moved=8 << 20,
    )(frames_in, cotangent, decay_rate)
    send = call(
        spread_body,
        "spread",
        shape((half, 112, lanes), BF),
        [VMEM] * 2,
        [
            pltpu.VMEM((2, 2, wide + 2 * PAD, lanes), F32),
            pltpu.VMEM((2, wide + 2 * PAD, lanes), F32),
        ],
    )(own, edge)
    mine = lax.all_to_all(send, "tm", 0, 0, axis_index_groups=groups)
    theirs = lax.ppermute(mine, "tm", swap)
    give, keep, stay = call(
        cell_body,
        "cells",
        (
            shape((half, share, 12 * lanes), BF),
            shape((half, share, 10 * lanes), F32),
            shape((half, 8, 2 * lanes), BF),
        ),
        [VMEM] * 6,
        [
            pltpu.VMEM((2 * sources, 2, 32, lanes), F32),
            pltpu.VMEM((2 * sources, 8, lanes), F32),
            pltpu.VMEM((sources, 8, lanes), F32),
            pltpu.VMEM((sources, 8, lanes), F32),
            pltpu.VMEM((cells, 9 * lanes), BF),
            pltpu.VMEM((cells, lanes), F32),
            pltpu.VMEM((cells, lanes), BF),
            pltpu.VMEM((cells, lanes), BF),
            pltpu.VMEM((cells, lanes), F32),
            pltpu.VMEM((lanes, cells), BF),
        ],
        flops=2 * cells * lanes * lanes * 21,
        moved=4 << 20,
    )(mine, theirs, kernel.reshape(9 * lanes, lanes), readout, begin, edge)
    taken = lax.ppermute(give, "tm", swap)
    send = call(merge_body, "merge", shape((half, share, 14 * lanes), BF), [VMEM] * 3, [])(taken, keep, stay)
    got = lax.all_to_all(send, "tm", 0, 0, axis_index_groups=groups)
    partial, drive, top = call(
        functools.partial(join_body, bands),
        "join",
        (
            shape((bands, share, 10 * block), BF),
            shape((2, 4, wide, lanes), BF),
            shape((2, 2, wide, lanes), BF),
        ),
        [VMEM],
        [pltpu.VMEM((8 * sources, 128), F32), pltpu.VMEM((wide, 128), F32)],
    )(got)
    below = lax.ppermute(top, "row", up)
    partial = lax.all_to_all(partial, "row", 0, 0)
    scaling = 1.0 / math.sqrt(here * sources * band_rows * bands * wide)
    partial = call(
        functools.partial(sum_body, scaling), "sum", shape((half, share, 10 * block), BF), [VMEM], []
    )(partial)

    def back(first, ins, **more):
        return call(
            functools.partial(back_body, first, bands),
            "back",
            shape(frames_in.shape, BF),
            ins,
            [
                pltpu.VMEM((2, 4, wide + 2 * PAD, lanes), F32),
                pltpu.VMEM((3, 2, 4, wide, lanes), BF),
                pltpu.VMEM((2, 2, wide, lanes), BF),
                pltpu.SemaphoreType.DMA,
            ],
            flops=cells * lanes * lanes * 9,
            moved=2 << 20,
            to=HBM,
            **more,
        )

    through = feedthrough.reshape(1, lanes)
    grad_frames = back(0, [VMEM] * 4)(drive, kernel, cotangent, through)
    grad_frames = back(2, [VMEM] * 5 + [HBM], alias={5: 0})(
        drive, below, kernel, cotangent, through, grad_frames
    )
    whole = lax.all_to_all(partial, "tm", 0, 0, axis_index_groups=groups)
    whole, grad_frames = lax.optimization_barrier((whole, grad_frames))
    other = lax.ppermute(whole, "tm", swap)
    grad_kernel, grad_readout = call(
        last_body, "last", (shape((9, block, lanes), F32), shape((block, lanes), F32)), [VMEM] * 2, []
    )(whole, other)
    return grad_frames, grad_kernel, grad_readout.T


def solution(mesh):
    placed = (
        P("tm", "row", None, None),
        P("tm", "row", None, None),
        P(),
        P(),
        P(),
        P("tm", None),
        P("row", None, None),
    )
    return jax.shard_map(
        local,
        mesh=mesh,
        in_specs=placed,
        out_specs=(P("tm", "row", None, None), P(None, "row", None), P(None, "row")),
        check_vma=False,
    )
```
